128 devices in a mesh: dp: 8 (over x, z_lo), ctx: 16 (over z_hi, y, core).
Axes of the slice: x: 4, y: 4, z: 4 (z_hi: 2, z_lo: 2; z = z_hi * 2 + z_lo), core: 2. Of those that a mesh axis runs over, the one named last changes fastest.
Arguments:
- tokens: bfloat16 [8, 8192, 1024], P('dp', 'ctx'), may hold values from -900 to 900
- grad_output: bfloat16 [8, 8192, 1024], P('dp', 'ctx'), may hold values from -6 to 6
- session_ids: int32 [8], P('dp'), may hold values from 0 to 63
- session_table: bfloat16 [64, 1024], replicated, may hold values from -6 to 6
- norm_gain: bfloat16 [1024], P('dp'), may hold values from 0.099609375 to 1.8984375
- input_weight: bfloat16 [1024, 2304], P('dp'), may hold values from -0.1875 to 0.1875
- step_weight: bfloat16 [1024, 16], P('dp'), may hold values from -1 to 1
- head_params: float32 [3, 16], replicated, may hold values from -9 to 4
- gate_gain: bfloat16 [1024], P('dp'), may hold values from 0.099609375 to 1.8984375
- output_weight: bfloat16 [1024, 1024], P('dp'), may hold values from -0.1875 to 0.1875
Outputs:
- tokens_grad: bfloat16 [8, 8192, 1024], P('dp', 'ctx')
- norm_grad: float32 [1024], P(('dp', 'ctx'))
- input_grad: float32 [1024, 2304], P(('dp', 'ctx'))
- step_grad: float32 [1024, 16], P(('dp', 'ctx'))
- head_grad: float32 [3, 16], replicated
- gate_grad: float32 [1024], P(('dp', 'ctx'))
- output_grad: float32 [1024, 1024], P(('dp', 'ctx'))
- table_grad: float32 [64, 1024], P(None, ('dp', 'ctx'))
The draws below stay inside these ranges and needn't reach their ends.
All inputs are finite; a program needn't handle non-finite values.
Results may differ from the reference program's by a relative error of at most 0.005.
The reference program's roundings to bfloat16 on the way (of `norm_act`, `mixed_out` and `grad_proj`) count: a program that leaves them out, or rounds other values in their place, can miss the bound.
Values may be sent and summed in bfloat16 or wider, within the bound.
No kernel may reach another device: no remote copies, remote signals or barrier semaphores. Data moves between devices by JAX's collectives and lax.ppermute only.
A program may use at most 128 MiB of HBM per device.

```python
import math
import jax
import jax.numpy as jnp
from jax import lax

D = 1024
HEADS = 16
HEAD = 64
STATE = 128
SESSIONS = 64
BINS_DEV = 512
INNER = 1024
PROJ = 2304
BATCH = 8
LENGTH = 8192


def volley_bearing(key):
    return jnp.clip(jax.random.normal(jax.random.fold_in(key, 7), (D,), jnp.float32), -4.0, 4.0)


def draw_tokens(key, part):
    derivative_trial_arrow = volley_bearing(key)
    keys = jax.random.split(jax.random.fold_in(key, 11), 5)
    gaussian_disturbance = jnp.clip(jax.random.normal(keys[0], (BATCH, LENGTH, D), jnp.float32), -4.0, 4.0)
    lateral_coefficient = jnp.exp(jax.random.uniform(keys[1], (BATCH, LENGTH, 1), jnp.float32, 0.0, math.log(10.0)))
    upright_coefficient = jnp.exp(jax.random.uniform(keys[2], (1, 1, D), jnp.float32, 0.0, math.log(10.0)))
    finite_step_length = jax.random.uniform(keys[3], (BATCH, LENGTH // 256, 1), jnp.float32, 0.0, 0.5)
    finite_step_length = jnp.repeat(finite_step_length, 256, axis=1)
    spots = jax.random.randint(keys[4], (BATCH, 3), 0, LENGTH)
    concordant_cases = jnp.arange(LENGTH)[None, :, None] == spots[:, None, :]
    neuron_discharge_train = jnp.any(concordant_cases, axis=-1).astype(jnp.float32)[:, :, None]
    quantity_items = lateral_coefficient * (upright_coefficient * gaussian_disturbance + (finite_step_length + 10.0 * neuron_discharge_train) * derivative_trial_arrow[None, None, :])
    return quantity_items.astype(jnp.bfloat16)


def draw_step_weight(key, part):
    derivative_trial_arrow = volley_bearing(key)
    gaussian_disturbance = jnp.clip(jax.random.normal(jax.random.fold_in(key, 13), (D, HEADS), jnp.float32), -4.0, 4.0)
    quantity_items = gaussian_disturbance / math.sqrt(D) + derivative_trial_arrow[:, None] * (10.0 / D)
    return quantity_items.astype(jnp.bfloat16)


def draw_head_params(key, part):
    keys = jax.random.split(jax.random.fold_in(key, 17), 5)
    bias = jax.random.uniform(keys[0], (HEADS,), jnp.float32, -8.5, -7.5)
    slow = math.log(1.0 / (LENGTH * 0.001))
    fast = math.log(1.0 / (40.0 * 0.001))
    lower = jax.random.uniform(keys[1], (HEADS,), jnp.float32, slow, slow + 0.7)
    upper = jax.random.uniform(keys[2], (HEADS,), jnp.float32, slow + 0.7, fast)
    picked = jax.random.bernoulli(keys[3], 0.5, (HEADS,))
    log_rate = jnp.where(picked, lower, upper)
    skip = jax.random.uniform(keys[4], (HEADS,), jnp.float32, 0.5, 1.5)
    return jnp.stack([bias, log_rate, skip]).astype(jnp.float32)


def place_ends(entries, stream_key, smallest, largest):
    extent = entries.shape
    spot = [jax.random.randint(jax.random.fold_in(stream_key, axis), (), 0, extent[axis]) for axis in range(len(extent))]
    entries = entries.at[tuple(spot)].set(smallest)
    longest = extent.index(max(extent))
    spot[longest] = (spot[longest] + 1) % extent[longest]
    return entries.at[tuple(spot)].set(largest)


def block_scale(stream_key, extent, shards, least, high):
    factor_of = 1.0
    for dim, shards_of in shards:
        steps = jax.random.uniform(jax.random.fold_in(jax.random.fold_in(stream_key, 6), dim), (shards_of,), jnp.float32, least / len(shards), high / len(shards))
        factor_of = factor_of * jnp.repeat(jnp.exp(steps), extent[dim] // shards_of).reshape((-1,) + (1,) * (len(extent) - 1 - dim))
    return factor_of


def centred(own_key, extent, scale, bound, shards=(), held_as=jnp.bfloat16):
    values = scale * jax.random.normal(own_key, extent, jnp.float32)
    if shards:
        values = values * block_scale(own_key, extent, shards, -0.22, 0.18)
    return jnp.clip(values, -bound, bound).astype(held_as)


def setup_inputs(seed: int = 0) -> dict:
    key_of = jax.random.split(jax.random.key(seed), 11)
    tokens = draw_tokens(jax.random.fold_in(key_of[10], 71), 0)
    grad_output = centred(key_of[1], (BATCH, LENGTH, D), 1.0, 6.0, ((0, 8), (1, 16)))
    session_ids = place_ends(jax.random.randint(key_of[2], (BATCH,), 0, SESSIONS), jax.random.fold_in(key_of[2], 1), 0, SESSIONS - 1).astype(jnp.int32)
    session_table = centred(key_of[3], (SESSIONS, D), 1.0, 6.0)
    norm_gain = jnp.clip(1.0 + 0.18 * jax.random.normal(key_of[4], (D,), jnp.float32), 0.099609375, 1.8984375).astype(jnp.bfloat16)
    input_weight = centred(key_of[5], (D, PROJ), D ** -0.5, 0.1875, ((0, 8),))
    step_weight = draw_step_weight(jax.random.fold_in(key_of[10], 71), 0)
    head_params = draw_head_params(jax.random.fold_in(key_of[10], 71), 0)
    gate_gain = jnp.clip(1.0 + 0.18 * jax.random.normal(key_of[8], (INNER,), jnp.float32), 0.099609375, 1.8984375).astype(jnp.bfloat16)
    output_weight = centred(key_of[9], (INNER, D), INNER ** -0.5, 0.1875, ((0, 8),))
    return {"tokens": tokens, "grad_output": grad_output, "session_ids": session_ids, "session_table": session_table, "norm_gain": norm_gain, "input_weight": input_weight, "step_weight": step_weight, "head_params": head_params, "gate_gain": gate_gain, "output_weight": output_weight}


epsilon = 1e-05

def normalize(quantity_items):
    factor = lax.rsqrt(lax.optimization_barrier(jnp.mean(quantity_items * quantity_items, axis=-1, keepdims=True)) + epsilon)
    return (quantity_items * factor, factor)

def block_prep(value_raw, step_raw, head_params):
    length = value_raw.shape[0]
    num_heads = step_raw.shape[1]
    activated = jax.nn.silu(value_raw)
    step_size = jax.nn.softplus(step_raw + head_params[0][None, :])
    log_rate = -jnp.exp(head_params[1])[None, :] * step_size
    log_decay = jnp.cumsum(log_rate, axis=0)
    scaled_in = step_size[:, :, None] * activated.reshape(length, num_heads, -1)
    return (activated, log_decay, scaled_in)

def state_block(value_raw, in_map, out_map, step_raw, head_params, state_in):
    length = value_raw.shape[0]
    num_heads = step_raw.shape[1]
    activated, log_decay, scaled_in = block_prep(value_raw, step_raw, head_params)
    positions = jnp.arange(length)
    causal = positions[:, None] >= positions[None, :]
    decay_log = log_decay.T
    decay_gap = jnp.where(causal[None], decay_log[:, :, None] - decay_log[:, None, :], 0.0)
    mask_decay = jnp.where(causal[None], jnp.exp(decay_gap), 0.0)
    scores = jnp.dot(out_map, in_map.T, precision=lax.Precision.HIGHEST)
    weighted = mask_decay * scores[None]
    result = jnp.einsum('hqk,khp->qhp', weighted, scaled_in, precision=lax.Precision.HIGHEST)
    carried = jnp.einsum('qn,hpn->qhp', out_map, state_in, precision=lax.Precision.HIGHEST)
    result = result + jnp.exp(log_decay)[:, :, None] * carried
    result = result + head_params[2][None, :, None] * activated.reshape(length, num_heads, -1)
    decay_tail = jnp.exp(log_decay[-1][None, :] - log_decay)
    fresh = jnp.einsum('kh,khp,kn->hpn', decay_tail, scaled_in, in_map, precision=lax.Precision.HIGHEST)
    state_out = jnp.exp(log_decay[-1])[:, None, None] * state_in + fresh
    return (result.reshape(length, -1), state_out)

def sequence_core(value_raw, in_map, out_map, step_raw, head_params):
    blocks = value_raw.shape[0] // BINS_DEV

    def advance(carry, pieces):
        result, state_out = state_block(pieces[0], pieces[1], pieces[2], pieces[3], head_params, carry)
        return (state_out, result)
    pieces = (value_raw.reshape(blocks, BINS_DEV, -1), in_map.reshape(blocks, BINS_DEV, -1), out_map.reshape(blocks, BINS_DEV, -1), step_raw.reshape(blocks, BINS_DEV, -1))
    start = jnp.zeros((HEADS, HEAD, STATE), jnp.float32)
    ending, results = lax.scan(jax.checkpoint(advance), start, pieces)
    return results.reshape(value_raw.shape[0], -1)

def one_sequence(tokens_row, grad_row, table_row, norm_gain, input_weight, step_weight, head_params, gate_gain, output_weight):
    norm_wide = norm_gain.astype(jnp.float32)
    gate_wide = gate_gain.astype(jnp.float32)
    layer_in = tokens_row.astype(jnp.float32) + table_row.astype(jnp.float32)[None, :]
    normed, in_scale = normalize(layer_in)
    norm_act = (normed * norm_wide[None, :]).astype(jnp.bfloat16)
    projected = jnp.dot(norm_act, input_weight, preferred_element_type=jnp.float32)
    step_raw = jnp.dot(norm_act, step_weight, preferred_element_type=jnp.float32)
    gate_pre = projected[:, :INNER]
    value_raw = projected[:, INNER:2 * INNER]
    in_map = projected[:, 2 * INNER:2 * INNER + STATE]
    out_map = projected[:, 2 * INNER + STATE:]
    ssd_out, core_back = jax.vjp(sequence_core, value_raw, in_map, out_map, step_raw, head_params)
    gated = ssd_out * jax.nn.silu(gate_pre)
    gated_norm, gate_scale = normalize(gated)
    mixed_out = (gated_norm * gate_wide[None, :]).astype(jnp.bfloat16)
    grad_mixed = jnp.dot(grad_row, output_weight.T, preferred_element_type=jnp.float32)
    term_output = jnp.dot(mixed_out.T, grad_row, preferred_element_type=jnp.float32)
    term_gate = lax.optimization_barrier(jnp.sum(grad_mixed * gated_norm, axis=0))
    grad_gnorm = grad_mixed * gate_wide[None, :]
    grad_gated = gate_scale * (grad_gnorm - gated_norm * lax.optimization_barrier(jnp.mean(grad_gnorm * gated_norm, axis=-1, keepdims=True)))
    gate_sig = jax.nn.sigmoid(gate_pre)
    grad_ssd = grad_gated * jax.nn.silu(gate_pre)
    grad_gate = grad_gated * ssd_out * gate_sig * (1.0 + gate_pre * (1.0 - gate_sig))
    grad_value, grad_in_map, grad_out_map, grad_step_raw, grad_heads = core_back(grad_ssd)
    grad_proj = jnp.concatenate([grad_gate, grad_value, grad_in_map, grad_out_map], axis=1).astype(jnp.bfloat16)
    grad_step_low = grad_step_raw.astype(jnp.bfloat16)
    grad_act = jnp.dot(grad_proj, input_weight.T, preferred_element_type=jnp.float32)
    grad_act = grad_act + jnp.dot(grad_step_low, step_weight.T, preferred_element_type=jnp.float32)
    term_input = jnp.dot(norm_act.T, grad_proj, preferred_element_type=jnp.float32)
    term_step = jnp.dot(norm_act.T, grad_step_low, preferred_element_type=jnp.float32)
    term_norm = lax.optimization_barrier(jnp.sum(grad_act * normed, axis=0))
    grad_normed = grad_act * norm_wide[None, :]
    grad_input = in_scale * (grad_normed - normed * lax.optimization_barrier(jnp.mean(grad_normed * normed, axis=-1, keepdims=True)))
    terms = (term_norm, term_input, term_step, grad_heads, term_gate, term_output, lax.optimization_barrier(jnp.sum(grad_input, axis=0)))
    return (grad_input.astype(jnp.bfloat16), terms)

def reference(tokens, grad_output, session_ids, session_table, norm_gain, input_weight, step_weight, head_params, gate_gain, output_weight):
    table_rows = session_table[session_ids]

    def per_sequence(pieces):
        return one_sequence(pieces[0], pieces[1], pieces[2], norm_gain, input_weight, step_weight, head_params, gate_gain, output_weight)
    tokens_grad, terms = lax.map(per_sequence, (tokens, grad_output, table_rows))
    grad_scale = 1.0 / math.sqrt(BATCH * LENGTH)
    totals = [lax.optimization_barrier(jnp.sum(term, axis=0)) * grad_scale for term in terms[:6]]
    session_hot = (session_ids[:, None] == jnp.arange(SESSIONS)[None, :]).astype(jnp.float32)
    table_grad = jnp.dot(session_hot.T, terms[6], precision=lax.Precision.HIGHEST) * grad_scale
    return (tokens_grad, totals[0], totals[1], totals[2], totals[3], totals[4], totals[5], table_grad)
```

```python
import math

import jax
import jax.numpy as jnp
from jax import lax
from jax.sharding import PartitionSpec as P

epsilon = 1e-05


ALL = ("dp", "ctx")


def core_partner(value):
    flips = [(i, i ^ 1) for i in range(lax.axis_size("dp") * lax.axis_size("ctx"))]
    return lax.ppermute(value, ALL, flips)


def on_first_core():
    return lax.axis_index("ctx") % 2 == 0


def gather_rows(shard):
    half = shard.shape[0] // 2
    count = lax.axis_size("dp")
    mine = jnp.where(on_first_core(), shard[:half], shard[half:])
    pieces = lax.all_to_all(jnp.broadcast_to(mine[None], (count,) + mine.shape), "dp", 0, 0)
    others = core_partner(pieces)
    low = jnp.where(on_first_core(), pieces, others)
    high = jnp.where(on_first_core(), others, pieces)
    return jnp.stack([low, high], axis=1).reshape(count * 2 * half, -1)


def carried_in(decay_total, state_local, backward):
    heads, rows, width = state_local.shape
    count = lax.axis_size("ctx")
    spread = jnp.broadcast_to(decay_total[:, None, None], (heads, 8, width))
    pieces = lax.all_to_all(jnp.concatenate([state_local, spread], axis=1), "ctx", 0, 0)
    order = range(count - 1, -1, -1) if backward else range(count)
    held = jnp.zeros((rows, width), jnp.float32)
    outs = [None] * count
    for place in order:
        outs[place] = held
        held = pieces[place, rows : rows + 1] * held + pieces[place, :rows]
    return lax.all_to_all(jnp.stack(outs), "ctx", 0, 0)


def scatter_sums(term_wide, extras):
    devices = lax.axis_size("dp") * lax.axis_size("ctx")
    packed = term_wide.astype(jnp.bfloat16)
    half = packed.shape[1] // 2
    mine = jnp.where(on_first_core(), packed[:, :half], packed[:, half:])
    other = jnp.where(on_first_core(), packed[:, half:], packed[:, :half])
    chip = mine.astype(jnp.float32) + core_partner(other).astype(jnp.float32)
    chip = chip.astype(jnp.bfloat16).reshape(devices, -1, half)
    coarse = extras.astype(jnp.bfloat16)
    fine = (extras - coarse.astype(jnp.float32)).astype(jnp.bfloat16)
    small = jnp.concatenate([coarse, fine], axis=1).reshape(devices, -1, 128)
    pieces = lax.all_to_all(jnp.concatenate([chip, small], axis=2), ALL, 0, 0)
    pieces = pieces.astype(jnp.float32)
    wide = jnp.sum(pieces[:, :, :half].reshape(devices // 2, 2, -1, half), axis=0)
    small = pieces[:, :, half : half + 64] + pieces[:, :, half + 64 :]
    return jnp.concatenate([wide[0], wide[1]], axis=1), small


def normalize(quantity_items):
    factor = lax.rsqrt(jnp.mean(quantity_items * quantity_items, axis=-1, keepdims=True) + epsilon)
    return (quantity_items * factor, factor)


def block_prep(value_raw, step_raw, head_params):
    length = value_raw.shape[0]
    num_heads = step_raw.shape[1]
    activated = jax.nn.silu(value_raw)
    step_size = jax.nn.softplus(step_raw + head_params[0][None, :])
    log_rate = -jnp.exp(head_params[1])[None, :] * step_size
    log_decay = jnp.cumsum(log_rate, axis=0)
    scaled_in = step_size[:, :, None] * activated.reshape(length, num_heads, -1)
    return (activated, log_decay, scaled_in)


def state_block(value_raw, in_map, out_map, step_raw, head_params, state_in):
    length = value_raw.shape[0]
    num_heads = step_raw.shape[1]
    activated, log_decay, scaled_in = block_prep(value_raw, step_raw, head_params)
    positions = jnp.arange(length)
    causal = positions[:, None] >= positions[None, :]
    decay_log = log_decay.T
    decay_gap = jnp.where(causal[None], decay_log[:, :, None] - decay_log[:, None, :], 0.0)
    mask_decay = jnp.where(causal[None], jnp.exp(decay_gap), 0.0)
    scores = jnp.dot(out_map, in_map.T, precision=lax.Precision.HIGHEST)
    weighted = mask_decay * scores[None]
    result = jnp.einsum("hqk,khp->qhp", weighted, scaled_in, precision=lax.Precision.HIGHEST)
    carried = jnp.einsum("qn,hpn->qhp", out_map, state_in, precision=lax.Precision.HIGHEST)
    result = result + jnp.exp(log_decay)[:, :, None] * carried
    result = result + head_params[2][None, :, None] * activated.reshape(length, num_heads, -1)
    decay_tail = jnp.exp(log_decay[-1][None, :] - log_decay)
    fresh = jnp.einsum(
        "kh,khp,kn->hpn", decay_tail, scaled_in, in_map, precision=lax.Precision.HIGHEST
    )
    state_out = jnp.exp(log_decay[-1])[:, None, None] * state_in + fresh
    return (result.reshape(length, -1), state_out)


def blocks_all(value_raw, in_map, out_map, step_raw, head_params, state_in):

    def per_sequence(pieces):
        return state_block(pieces[0], pieces[1], pieces[2], pieces[3], head_params, pieces[4])

    runner = jax.checkpoint(per_sequence)
    return lax.map(runner, (value_raw, in_map, out_map, step_raw, state_in))


def per_device(
    tokens,
    grad_output,
    session_ids,
    session_table,
    norm_gain,
    input_weight,
    step_weight,
    head_params,
    gate_gain,
    output_weight,
):
    shard = jnp.concatenate(
        [
            input_weight,
            step_weight,
            norm_gain[:, None],
            gate_gain[:, None],
            jnp.zeros((input_weight.shape[0], 110), jnp.bfloat16),
            output_weight,
        ],
        axis=1,
    )
    whole = gather_rows(shard)
    wide = input_weight.shape[1]
    input_full = whole[:, :wide]
    step_full = whole[:, wide : wide + 16]
    norm_low = whole[:, wide + 16]
    gate_low = whole[:, wide + 17]
    output_full = whole[:, wide + 128 :]
    norm_full = norm_low.astype(jnp.float32)
    gate_full = gate_low.astype(jnp.float32)
    num_seqs, num_bins, model_width = tokens.shape
    inner_width = output_full.shape[0]
    state_width = (input_full.shape[1] - 2 * inner_width) // 2
    num_heads = step_full.shape[1]
    sessions = session_table.shape[0]
    grad_scale = 1.0 / math.sqrt(num_seqs * num_bins * lax.axis_size("dp") * lax.axis_size("ctx"))
    session_hot = (session_ids[:, None] == jnp.arange(sessions)[None, :]).astype(jnp.float32)
    table_rows = jnp.dot(
        session_hot, session_table.astype(jnp.float32), precision=lax.Precision.HIGHEST
    )
    layer_in = tokens.astype(jnp.float32) + table_rows[:, None, :]
    normed, in_scale = normalize(layer_in)
    norm_act = (normed * norm_full[None, None, :]).astype(jnp.bfloat16)
    projected = jnp.einsum("sqd,de->sqe", norm_act, input_full, preferred_element_type=jnp.float32)
    step_raw = jnp.einsum("sqd,dh->sqh", norm_act, step_full, preferred_element_type=jnp.float32)
    gate_pre = projected[:, :, :inner_width]
    value_raw = projected[:, :, inner_width : 2 * inner_width]
    in_map = projected[:, :, 2 * inner_width : 2 * inner_width + state_width]
    out_map = projected[:, :, 2 * inner_width + state_width :]
    activated, log_decay, scaled_in = jax.vmap(block_prep, in_axes=(0, 0, None))(
        value_raw, step_raw, head_params
    )
    decay_total = jnp.exp(log_decay[:, -1, :])
    decay_tail = jnp.exp(log_decay[:, -1:, :] - log_decay)
    state_local = jnp.einsum(
        "skh,skhp,skn->shpn", decay_tail, scaled_in, in_map, precision=lax.Precision.HIGHEST
    )
    state_in = carried_in(decay_total[0], state_local[0], False)[None]
    outputs, core_back = jax.vjp(
        blocks_all, value_raw, in_map, out_map, step_raw, head_params, state_in
    )
    ssd_out = outputs[0]
    gated = ssd_out * jax.nn.silu(gate_pre)
    gated_norm, gate_scale = normalize(gated)
    mixed_out = (gated_norm * gate_full[None, None, :]).astype(jnp.bfloat16)
    grad_mixed = jnp.einsum(
        "sqd,ed->sqe", grad_output, output_full, preferred_element_type=jnp.float32
    )
    term_output = (
        jnp.einsum("sqe,sqd->ed", mixed_out, grad_output, preferred_element_type=jnp.float32)
        * grad_scale
    )
    term_gate = jnp.sum(grad_mixed * gated_norm, axis=(0, 1)) * grad_scale
    grad_gnorm = grad_mixed * gate_full[None, None, :]
    grad_gated = gate_scale * (
        grad_gnorm - gated_norm * jnp.mean(grad_gnorm * gated_norm, axis=-1, keepdims=True)
    )
    gate_sig = jax.nn.sigmoid(gate_pre)
    grad_ssd = grad_gated * jax.nn.silu(gate_pre)
    grad_gate = grad_gated * ssd_out * gate_sig * (1.0 + gate_pre * (1.0 - gate_sig))
    heads_view = grad_ssd.reshape(num_seqs, num_bins, num_heads, -1)
    adjoint_local = jnp.einsum(
        "sqh,sqhp,sqn->shpn",
        jnp.exp(log_decay),
        heads_view,
        out_map,
        precision=lax.Precision.HIGHEST,
    )
    adjoint_out = carried_in(decay_total[0], adjoint_local[0], True)[None]
    grad_value, grad_in_map, grad_out_map, grad_step_raw, grad_heads, unused_state = core_back(
        (grad_ssd, adjoint_out)
    )
    grad_proj = jnp.concatenate([grad_gate, grad_value, grad_in_map, grad_out_map], axis=2).astype(
        jnp.bfloat16
    )
    grad_step_low = grad_step_raw.astype(jnp.bfloat16)
    grad_act = jnp.einsum("sqe,de->sqd", grad_proj, input_full, preferred_element_type=jnp.float32)
    grad_act = grad_act + jnp.einsum(
        "sqh,dh->sqd", grad_step_low, step_full, preferred_element_type=jnp.float32
    )
    term_input = (
        jnp.einsum("sqd,sqe->de", norm_act, grad_proj, preferred_element_type=jnp.float32)
        * grad_scale
    )
    term_step = (
        jnp.einsum("sqd,sqh->dh", norm_act, grad_step_low, preferred_element_type=jnp.float32)
        * grad_scale
    )
    term_norm = jnp.sum(grad_act * normed, axis=(0, 1)) * grad_scale
    grad_normed = grad_act * norm_full[None, None, :]
    grad_input = in_scale * (
        grad_normed - normed * jnp.mean(grad_normed * normed, axis=-1, keepdims=True)
    )
    rows, wide = term_input.shape
    table_row = jnp.sum(grad_input, axis=(0, 1)) * grad_scale
    head_rows = (grad_heads * grad_scale).reshape(8, 6)
    session = jnp.broadcast_to(session_ids.astype(jnp.float32)[:, None], (rows, 1))
    extras = jnp.concatenate(
        [
            term_step,
            term_norm[:, None],
            term_gate[:, None],
            jnp.tile(head_rows, (rows // 8, 1)),
            table_row[:, None],
            session,
            jnp.zeros((rows, 38), jnp.float32),
        ],
        axis=1,
    )
    sums, small = scatter_sums(jnp.concatenate([term_input, term_output], axis=1), extras)
    total = jnp.sum(small, axis=0)
    hot = (small[:, 0, 25][None, :] == jnp.arange(sessions)[:, None]).astype(jnp.float32)
    table_grad = jnp.dot(hot, small[:, :, 24], precision=lax.Precision.HIGHEST)
    return (
        grad_input.astype(jnp.bfloat16),
        total[:, 16],
        sums[:, :wide],
        total[:, :16],
        total[:, 18:24].reshape(3, 16),
        total[:, 17],
        sums[:, wide:],
        table_grad,
    )


def solution(mesh):
    placed = (
        P("dp", "ctx", None),
        P("dp", "ctx", None),
        P("dp"),
        P(),
        P("dp"),
        P("dp", None),
        P("dp", None),
        P(),
        P("dp"),
        P("dp", None),
    )
    return jax.shard_map(
        per_device,
        mesh=mesh,
        in_specs=placed,
        out_specs=(
            P("dp", "ctx", None),
            P(("dp", "ctx")),
            P(("dp", "ctx"), None),
            P(("dp", "ctx"), None),
            P(),
            P(("dp", "ctx")),
            P(("dp", "ctx"), None),
            P(None, ("dp", "ctx")),
        ),
        check_vma=False,
    )
```

```python
import functools
import math

import jax
import jax.numpy as jnp
from jax import lax
from jax.experimental import pallas as pl
from jax.experimental.pallas import tpu as pltpu
from jax.sharding import PartitionSpec as P

epsilon = 1e-05
ALL = ("dp", "ctx")
Q = 128
F32 = jnp.float32
LOW = jnp.bfloat16
NN = (((1,), (0,)), ((), ()))
NT = (((1,), (1,)), ((), ()))


def dot(a, b, dims=NN):
    return lax.dot_general(a, b, dims, preferred_element_type=F32)


def split(x):
    high = x.astype(LOW)
    return high, (x - high.astype(F32)).astype(LOW)


def dot3(a, b, dims=NN):
    (ah, al), (bh, bl) = split(a), split(b)
    return dot(ah, bh, dims) + dot(ah, bl, dims) + dot(al, bh, dims)


def thirds(x):
    high = x.astype(LOW)
    rest = x - high.astype(F32)
    mid = rest.astype(LOW)
    return high, mid, (rest - mid.astype(F32)).astype(LOW)


def select_dot(x, chosen, dims=NN):
    high, mid, low = thirds(x)
    return dot(high, chosen, dims) + dot(mid, chosen, dims) + dot(low, chosen, dims)


def select_left(chosen, x):
    high, mid, low = thirds(x)
    return dot(chosen, high) + dot(chosen, mid) + dot(chosen, low)


def sigmoid(x):
    return 1.0 / (1.0 + jnp.exp(-x))


def softplus(x):
    u = jnp.exp(-jnp.abs(x))
    w = 1.0 + u
    log1p = jnp.where(w == 1.0, u, jnp.log(w) * (u / jnp.where(w == 1.0, 1.0, w - 1.0)))
    return jnp.maximum(x, 0.0) + log1p


def iota(dim, shape=(Q, Q)):
    return lax.broadcasted_iota(jnp.int32, shape, dim)


def rows_of(c):
    return pl.ds(pl.multiple_of(c * Q, Q), Q)


def assemble(core, mine, other, whole):
    half = mine.shape[1]
    first = pl.multiple_of(core * half, half)
    second = pl.multiple_of((1 - core) * half, half)
    for i in range(mine.shape[0]):
        whole[pl.ds(2 * half * i + first, half), :] = mine[i]
        whole[pl.ds(2 * half * i + second, half), :] = other[i]


def prep_kernel(
    core_ref, tok, row, mine, other, hp, spread,
    wide, act_low, scale, value, in_map, out_map, step_raw, step, decay, fresh, packed, gains,
    state, total,
):
    assemble(core_ref[0], mine, other, wide)
    small = wide[:, 1280:1408].astype(F32).T
    gains[0:1, :] = small[16:17, :]
    gains[1:2, :] = small[17:18, :]
    state[...] = jnp.zeros_like(state)
    total[...] = jnp.zeros_like(total)
    ones_low = (iota(0) >= iota(1)).astype(F32).astype(LOW)
    used = iota(1) < 16

    def body(c, carry):
        rows = rows_of(c)
        x = tok[rows, :].astype(F32) + row[0:1, :]
        factor = lax.rsqrt(jnp.mean(x * x, axis=1, keepdims=True) + epsilon)
        low = (x * factor * gains[0:1, :]).astype(LOW)
        act_low[rows, :] = low
        scale[rows, :] = jnp.broadcast_to(factor, (Q, 128))
        value_c = dot(low, wide[:, :1024])
        value[rows, :] = value_c
        rest = dot(low, wide[:, 1024:1408])
        in_c = rest[:, 0:128]
        in_map[rows, :] = in_c
        out_map[rows, :] = rest[:, 128:256]
        raw = jnp.where(used, rest[:, 256:384] + hp[0:1, :], 0.0)
        step_raw[rows, :] = raw
        size = jnp.where(used, softplus(raw), 0.0)
        step[rows, :] = size
        logs = select_left(ones_low, -jnp.exp(hp[1:2, :]) * size)
        decay[rows, :] = logs
        last = logs[Q - 1 : Q, :]
        weight = select_dot(jnp.exp(last - logs) * size, spread[...])
        activated = value_c * sigmoid(value_c)
        fresh_c = dot3(in_c.T, weight * activated)
        fresh[rows, :] = fresh_c
        through = select_dot(jnp.broadcast_to(jnp.exp(last), (8, 128)), spread[...])[0:1, :]
        state[...] = through * state[...] + fresh_c
        total[...] = total[...] + last
        return carry

    lax.fori_loop(0, tok.shape[0] // Q, body, 0)
    packed[:, :1024] = state[...]
    packed[:, 1024:1152] = jnp.broadcast_to(jnp.exp(total[0:1, :]), (128, 128))


def scan_forward(pieces, spread, carried, decays):
    count = pieces.shape[0]
    rates = jnp.concatenate([pieces[j, 0:1, 1024:1152] for j in range(count)], axis=0)
    decays[...] = select_dot(rates, spread[...])
    held = jnp.zeros((8, 1024), F32)
    for j in range(count):
        carried[j] = held
        held = decays[j : j + 1, :] * held + pieces[j, :, :1024]


def scan_backward(pieces, decays, carried):
    count = pieces.shape[0]
    held = jnp.zeros((8, 1024), F32)
    for j in range(count - 1, -1, -1):
        carried[j] = held
        held = decays[j : j + 1, :] * held + pieces[j]


def pair_gaps(logs, logs_t, pair, transposed):
    gaps = []
    for head in (2 * pair, 2 * pair + 1):
        column = jnp.broadcast_to(logs[:, head : head + 1], (Q, Q))
        across = jnp.broadcast_to(logs_t[head : head + 1, :], (Q, Q))
        if transposed:
            gap = jnp.where(iota(1) >= iota(0), across - column, -1e30)
        else:
            gap = jnp.where(iota(0) >= iota(1), column - across, -1e30)
        gaps.append(jnp.exp(gap))
    return gaps


def by_head(x, axis):
    first = iota(1) < 64
    return jnp.concatenate([jnp.where(first, x, 0.0), jnp.where(first, 0.0, x)], axis=axis)


def widen(row, spread):
    return select_dot(jnp.broadcast_to(row, (8, 128)), spread)[0:1, :]


def local_kernel(value, in_map, out_map, step, decay, fresh, spread, y_local, states, ssd, scaled, held):
    held[...] = jnp.zeros_like(held)

    def body(c, carry):
        rows = rows_of(c)
        states[rows, :] = held[...]
        logs = decay[rows, :]
        logs_t = logs.T
        value_c = value[rows, :]
        scaled[...] = select_dot(step[rows, :], spread[...]) * (value_c * sigmoid(value_c))
        reach = select_dot(jnp.exp(logs), spread[...])
        out_c = out_map[rows, :]
        scores = dot3(out_c, in_map[rows, :], NT)
        for pair in range(8):
            lanes = slice(128 * pair, 128 * pair + 128)
            one, two = pair_gaps(logs, logs_t, pair, False)
            weighted = jnp.concatenate([one * scores, two * scores], axis=1)
            ssd[:, lanes] = dot3(weighted, by_head(scaled[:, lanes], 0))
        y_local[rows, :] = ssd[...] + reach * dot3(out_c, held[...])
        through = widen(jnp.exp(logs[Q - 1 : Q, :]), spread[...])
        held[...] = through * held[...] + fresh[rows, :]
        return carry

    lax.fori_loop(0, value.shape[0] // Q, body, 0)


def mix_kernel(
    place_ref, act_low, mine, other, grad_out, value, out_map, decay, y_local,
    states_local, state_in, gains, hp, spread,
    gate_whole, mixed, grad_gate, grad_ssd, out_dot, adjoint, adjoint_local, states, sums,
    out_whole, base,
):
    core, group = place_ref[0], place_ref[1]
    half = mine.shape[1]
    for i in range(mine.shape[0]):
        start = ((group + i // 2) % 4 * 2 + i % 2) * (2 * half)
        for block, turn in ((mine, core), (other, 1 - core)):
            rows = pl.ds(pl.multiple_of(start + turn * half, half), half)
            gate_whole[rows, :] = block[i, :, :1024]
            out_whole[rows, :] = block[i, :, 1024:]
    base[...] = jnp.ones_like(base)
    adjoint_local[...] = jnp.zeros_like(adjoint_local)
    sums[...] = jnp.zeros_like(sums)
    skip = widen(hp[2:3, :], spread[...])

    def body(c, carry):
        rows = rows_of(c)
        before = base[0:1, :]
        entering = before * state_in[...]
        states[rows, :] = states_local[rows, :] + entering
        logs = decay[rows, :]
        value_c = value[rows, :]
        activated = value_c * sigmoid(value_c)
        reach = select_dot(jnp.exp(logs), spread[...])
        out_c = out_map[rows, :]
        y_state = y_local[rows, :] + reach * dot3(out_c, entering)
        y = y_state + skip * activated
        gate = dot(act_low[rows, :], gate_whole[...])
        grad_mixed = dot(grad_out[rows, :], out_whole[...], NT)
        sig = sigmoid(gate)
        silu = gate * sig
        gated = y * silu
        gate_scale = lax.rsqrt(jnp.mean(gated * gated, axis=1, keepdims=True) + epsilon)
        gnorm = gated * gate_scale
        mixed[rows, :] = (gnorm * gains[1:2, :]).astype(LOW)
        along = grad_mixed * gnorm
        sums[0:1, :] = sums[0:1, :] + jnp.sum(along, axis=0, keepdims=True)
        grad_gnorm = grad_mixed * gains[1:2, :]
        mean = jnp.mean(grad_gnorm * gnorm, axis=1, keepdims=True)
        grad_gated = gate_scale * (grad_gnorm - gnorm * mean)
        grad_gate[rows, :] = (grad_gated * y * sig * (1.0 + gate * (1.0 - sig))).astype(LOW)
        grad_y = grad_gated * silu
        grad_ssd[rows, :] = grad_y
        sums[1:2, :] = sums[1:2, :] + jnp.sum(grad_y * activated, axis=0, keepdims=True)
        out_dot[rows, :] = select_dot(grad_y * y_state, spread[...], NT)
        adjoint_c = dot3(out_c.T, reach * grad_y)
        adjoint[rows, :] = adjoint_c
        adjoint_local[...] = adjoint_local[...] + before * adjoint_c
        base[0:1, :] = before * widen(jnp.exp(logs[Q - 1 : Q, :]), spread[...])
        return carry

    lax.fori_loop(0, act_low.shape[0] // Q, body, 0)


def inner_kernel(
    spread, value, in_map, out_map, step, decay, fresh, states, grad_ssd, adjoint,
    grad_scaled, grad_maps, crossings,
    held, scaled,
):
    held[...] = jnp.zeros_like(held)
    chunks = value.shape[0] // Q

    def body(i, carry):
        c = chunks - 1 - i
        rows = rows_of(c)
        logs = decay[rows, :]
        logs_t = logs.T
        last = logs[Q - 1 : Q, :]
        in_c = in_map[rows, :]
        out_c = out_map[rows, :]
        through = widen(jnp.exp(last), spread[...])
        state_end = through * states[rows, :] + fresh[rows, :]
        crossing = jnp.sum(held[...] * state_end, axis=0, keepdims=True)
        crossing = select_dot(jnp.broadcast_to(crossing, (8, 1024)), spread[...], NT)
        crossings[pl.ds(pl.multiple_of(8 * c, 8), 8), :] = crossing
        value_c = value[rows, :]
        scaled[...] = select_dot(step[rows, :], spread[...]) * (value_c * sigmoid(value_c))
        tail = select_dot(jnp.exp(last - logs), spread[...])
        grad_scaled[rows, :] = tail * dot3(in_c, held[...])
        grad_in = dot3(tail * scaled[...], held[...], NT)
        reach = select_dot(jnp.exp(logs), spread[...])
        grad_out_map = dot3(reach * grad_ssd[rows, :], states[rows, :], NT)
        scores = dot3(in_c, out_c, NT)
        grad_scores = jnp.zeros((Q, Q), F32)
        for pair in range(8):
            lanes = slice(128 * pair, 128 * pair + 128)
            one, two = pair_gaps(logs, logs_t, pair, True)
            grad_pair = by_head(grad_ssd[rows, lanes], 0)
            weighted = jnp.concatenate([one * scores, two * scores], axis=1)
            grad_scaled[rows, lanes] = grad_scaled[rows, lanes] + dot3(weighted, grad_pair)
            both = dot3(scaled[:, lanes], grad_pair, NT)
            grad_scores = grad_scores + one * both[:, :Q] + two * both[:, Q:]
        grad_maps[rows, 0:128] = grad_in + dot3(grad_scores, out_c)
        grad_maps[rows, 128:256] = grad_out_map + dot3(grad_scores.T, in_c)
        held[...] = adjoint[rows, :] + through * held[...]
        return carry

    lax.fori_loop(0, chunks, body, 0)


def grad_kernel(
    tok, row, scale, gains, hp, spread, wide, gate_whole, grad_gate, value, in_map,
    step_raw, step, decay, fresh, states, grad_ssd, out_dot, grad_inner, grad_maps, crossings,
    adjoint_out, sums_mix,
    grad_wide, tokens_grad, sums, heads,
    after,
):
    after[...] = jnp.ones_like(after)
    sums[...] = jnp.zeros_like(sums)
    heads[...] = jnp.zeros_like(heads)
    heads[2:3, :] = select_dot(sums_mix[...], spread[...], NT)[1:2, :]
    skip = widen(hp[2:3, :], spread[...])
    chunks = tok.shape[0] // Q
    ones_up = (iota(1) >= iota(0)).astype(F32).astype(LOW)

    def body(i, carry):
        c = chunks - 1 - i
        rows = rows_of(c)
        logs = decay[rows, :]
        last = logs[Q - 1 : Q, :]
        size = step[rows, :]
        through = widen(jnp.exp(last), spread[...])
        leaving = after[0:1, :] * adjoint_out[...]
        state_end = through * states[rows, :] + fresh[rows, :]
        crossing = jnp.sum(leaving * state_end, axis=0, keepdims=True)
        crossing = select_dot(jnp.broadcast_to(crossing, (8, 1024)), spread[...], NT)
        crossing = (crossing + crossings[pl.ds(pl.multiple_of(8 * c, 8), 8), :])[0:1, :]
        value_c = value[rows, :]
        sig = sigmoid(value_c)
        activated = value_c * sig
        size_wide = select_dot(size, spread[...])
        tail = select_dot(jnp.exp(last - logs), spread[...])
        grad_scaled = grad_inner[rows, :] + tail * dot3(in_map[rows, :], leaving)
        grad_in = grad_maps[rows, 0:128] + dot3(tail * (size_wide * activated), leaving, NT)
        per_step = select_dot(activated * grad_scaled, spread[...], NT)
        grad_logs = out_dot[rows, :] - size * per_step
        grad_rate = select_left(ones_up, grad_logs) + crossing
        speed = jnp.exp(hp[1:2, :])
        raw = step_raw[rows, :]
        grad_raw = jnp.where(iota(1) < 16, (per_step - speed * grad_rate) * sigmoid(raw), 0.0)
        heads[0:1, :] = heads[0:1, :] + jnp.sum(grad_raw, axis=0, keepdims=True)
        heads[1:2, :] = heads[1:2, :] - jnp.sum(
            grad_rate * (speed * size), axis=0, keepdims=True
        )
        grad_act_c = size_wide * grad_scaled + skip * grad_ssd[rows, :]
        grad_wide[rows, 0:1024] = (grad_act_c * sig * (1.0 + value_c * (1.0 - sig))).astype(LOW)
        grad_wide[rows, 1024:1152] = grad_in.astype(LOW)
        grad_wide[rows, 1152:1280] = grad_maps[rows, 128:256].astype(LOW)
        grad_wide[rows, 1280:1408] = grad_raw.astype(LOW)
        after[0:1, :] = after[0:1, :] * through
        grad_act = dot(grad_wide[rows, :], wide[...], NT) + dot(
            grad_gate[rows, :], gate_whole[...], NT
        )
        factor = scale[rows, 0:1]
        normed = (tok[rows, :].astype(F32) + row[0:1, :]) * factor
        sums[0:1, :] = sums[0:1, :] + jnp.sum(grad_act * normed, axis=0, keepdims=True)
        grad_normed = grad_act * gains[0:1, :]
        mean = jnp.mean(grad_normed * normed, axis=1, keepdims=True)
        grad_input = factor * (grad_normed - normed * mean)
        tokens_grad[rows, :] = grad_input.astype(LOW)
        sums[1:2, :] = sums[1:2, :] + jnp.sum(grad_input, axis=0, keepdims=True)
        return carry

    lax.fori_loop(0, chunks, body, 0)


def early_kernel(mine, other, packed):
    def body(j, carry):
        rows = pl.ds(pl.multiple_of(j * Q, Q), Q)
        both = mine[rows, :].astype(F32) + other[rows, :].astype(F32)
        packed[pl.ds(j * 16, 16)] = both.reshape(16, 8, -1).astype(LOW)
        return carry

    lax.fori_loop(0, mine.shape[0] // Q, body, 0)


def late_kernel(core_ref, term, other, sums, sums_mix, tile, packed, across, columns):
    across[...] = jnp.zeros_like(across)
    across[16:17, :] = sums[0:1, :]
    across[17:18, :] = sums_mix[0:1, :]
    across[24:25, :] = sums[1:2, :]
    columns[...] = across[...].T
    first = core_ref[0] == 0
    lane = iota(1)

    def body(j, carry):
        rows = pl.ds(pl.multiple_of(j * Q, Q), Q)
        mine = jnp.where(first, term[rows, 0:640], term[rows, 640:1280])
        both = mine.astype(LOW).astype(F32) + other[rows, :].astype(F32)
        packed[pl.ds(j * 16, 16), :, 0:640] = both.reshape(16, 8, 640).astype(LOW)
        extra = (term[rows, 1280:1408] + columns[rows, :]).reshape(16, 8, 128)
        extra = (extra + tile[...][None]).reshape(Q, 128)
        coarse = extra.astype(LOW).astype(F32)
        fine = pltpu.roll(extra - coarse, 64, 1)
        small = jnp.where(lane < 64, coarse, fine)
        packed[pl.ds(j * 16, 16), :, 640:768] = small.reshape(16, 8, 128).astype(LOW)
        return carry

    lax.fori_loop(0, term.shape[0] // Q, body, 0)


def sum_kernel(grad_scale, early, late, input_grad, output_grad, small, table):
    input_grad[...] = jnp.zeros_like(input_grad)
    output_grad[...] = jnp.zeros_like(output_grad)
    small[...] = jnp.zeros_like(small)
    table[...] = jnp.zeros_like(table)
    lane = lax.broadcasted_iota(jnp.int32, (8, 128), 1).astype(F32)

    def body(j, carry):
        input_grad[:, 0:1024] += early[2 * j].astype(F32)
        output_grad[...] += early[2 * j + 1].astype(F32)
        input_grad[:, 1024:1664] += late[2 * j, :, 0:640].astype(F32)
        input_grad[:, 1664:2304] += late[2 * j + 1, :, 0:640].astype(F32)
        for k in range(2):
            parts = late[2 * j + k, :, 640:768].astype(F32)
            parts = parts + pltpu.roll(parts, 64, 1)
            small[...] += parts
            table[...] += jnp.where(lane == parts[:, 25:26], parts[:, 24:25], 0.0)
        return carry

    lax.fori_loop(0, early.shape[0] // 2, body, 0, unroll=4)
    for out in (input_grad, output_grad, small, table):
        out[...] = out[...] * grad_scale


def at_origin(rank, *unused):
    return (0,) * rank


def run(kernel, args, outs, scratch=(), scalars=0):
    specs = [
        pl.BlockSpec(
            arg.shape, functools.partial(at_origin, arg.ndim), pipeline_mode=pl.Buffered(1)
        )
        for arg in args[scalars:]
    ]
    out_specs = [
        pl.BlockSpec(shape, functools.partial(at_origin, len(shape)), pipeline_mode=pl.Buffered(1))
        for shape, _ in outs
    ]
    return pl.pallas_call(
        kernel,
        name=getattr(kernel, "__name__", "sum_kernel"),
        out_shape=[jax.ShapeDtypeStruct(shape, dtype) for shape, dtype in outs],
        grid_spec=pltpu.PrefetchScalarGridSpec(
            num_scalar_prefetch=scalars,
            grid=(1,),
            in_specs=specs,
            out_specs=out_specs,
            scratch_shapes=[pltpu.VMEM(shape, dtype) for shape, dtype in scratch],
        ),
        compiler_params=pltpu.CompilerParams(vmem_limit_bytes=60 << 20),
    )(*args)


def core_partner(value):
    flips = [(i, i ^ 1) for i in range(lax.axis_size("dp") * lax.axis_size("ctx"))]
    return lax.ppermute(value, ALL, flips)


def on_first_core():
    return lax.axis_index("ctx") % 2 == 0


def gather_rows(shard):
    half = shard.shape[0] // 2
    count = lax.axis_size("dp")
    mine = jnp.where(on_first_core(), shard[:half], shard[half:])
    pieces = lax.all_to_all(jnp.broadcast_to(mine[None], (count,) + mine.shape), "dp", 0, 0)
    return pieces, core_partner(pieces)


def moved(value, to):
    count = lax.axis_size("dp") * lax.axis_size("ctx")
    return lax.ppermute(value, ALL, [(i, to(i) % count) for i in range(count)])


def ring_near(shard):
    half = shard.shape[0] // 2
    slots = lax.axis_size("ctx")
    mine = jnp.where(on_first_core(), shard[:half], shard[half:])
    return mine, moved(mine, lambda i: i ^ slots)


def ring_sides(mine, near):
    step = 2 * lax.axis_size("ctx")
    even = lax.axis_index("dp") % 2 == 0
    pair = jnp.stack([jnp.where(even, mine, near), jnp.where(even, near, mine)])
    return pair, moved(pair, lambda i: i + step), moved(pair, lambda i: i - step)


def ring_far(lower, upper):
    step = 2 * lax.axis_size("ctx")
    half = lower.shape[1] // 2
    far_low = moved(lower[:, :half], lambda i: i + step)
    far_high = moved(upper[:, half:], lambda i: i - step)
    return far_low, far_high


def column_dot(a, b):
    return lax.dot_general(a, b, (((0,), (0,)), ((), ())), preferred_element_type=F32)


def per_device(
    tokens,
    grad_output,
    session_ids,
    session_table,
    norm_gain,
    input_weight,
    step_weight,
    head_params,
    gate_gain,
    output_weight,
):
    tok, grad_out = tokens[0], grad_output[0]
    bins = tok.shape[0]
    devices = lax.axis_size("dp") * lax.axis_size("ctx")
    slots = lax.axis_size("ctx")
    sessions = session_table.shape[0]
    grad_scale = 1.0 / math.sqrt(bins * devices)
    core = (lax.axis_index("ctx") % 2).astype(jnp.int32)[None]
    first = on_first_core()
    row = lax.dynamic_slice(session_table, (session_ids[0], 0), (1, 1024)).astype(F32)
    row = jnp.broadcast_to(row, (8, 1024))
    params = jnp.pad(head_params, ((0, 5), (0, 112)))
    spread = (jnp.arange(1024)[None, :] // 64 == jnp.arange(128)[:, None]).astype(LOW)
    shard = jnp.concatenate(
        [
            input_weight[:, 1024:],
            step_weight,
            norm_gain[:, None],
            gate_gain[:, None],
            jnp.zeros((input_weight.shape[0], 110), LOW),
        ],
        axis=1,
    )
    mine, other = gather_rows(shard)
    mine, rest = lax.optimization_barrier(
        (mine, jnp.concatenate([input_weight[:, :1024], output_weight], axis=1))
    )
    rest_half, near = ring_near(rest)
    place = jnp.stack([core[0], lax.axis_index("dp").astype(jnp.int32) // 2])
    seq = (bins, 1024)
    lane = (bins, 128)
    prepared = run(
        prep_kernel,
        (core, tok, row, mine, other, params, spread),
        (
            ((1024, 1408), LOW), (seq, LOW), (lane, F32), (seq, F32), (lane, F32), (lane, F32),
            (lane, F32), (lane, F32), (lane, F32), (seq, F32), ((128, 1152), F32), ((8, 1024), F32),
        ),
        (((128, 1024), F32), ((8, 128), F32)),
        1,
    )
    wide, act_low, scale, value, in_map, out_map, step_raw, step, decay, fresh, packed, gains = (
        prepared
    )
    near, packed = lax.optimization_barrier((near, packed))
    pair, lower, upper = ring_sides(rest_half, near)
    pieces = lax.all_to_all(packed.reshape(slots, 8, 1152), "ctx", 0, 0)
    y_local, states_local = run(
        local_kernel,
        (value, in_map, out_map, step, decay, fresh, spread),
        ((seq, F32), (seq, F32)),
        (((Q, 1024), F32), ((Q, 1024), F32), ((128, 1024), F32)),
    )
    pieces, y_local, lower, upper = lax.optimization_barrier((pieces, y_local, lower, upper))
    far_low, far_high = ring_far(lower, upper)
    carried, decays = run(
        scan_forward, (pieces, spread), (((slots, 8, 1024), F32), ((slots, 1024), F32))
    )
    carried, far_low, far_high = lax.optimization_barrier((carried, far_low, far_high))
    far = jnp.concatenate([far_low, far_high], axis=1)
    rest_mine = jnp.concatenate([pair, upper, far, lower], axis=0)
    rest_other = core_partner(rest_mine)
    state_in = lax.all_to_all(carried, "ctx", 0, 0).reshape(128, 1024)
    gate_whole, mixed, grad_gate, grad_ssd, out_dot, adjoint, adjoint_local, states, sums_mix = run(
        mix_kernel,
        (
            place, act_low, rest_mine, rest_other, grad_out, value, out_map, decay, y_local,
            states_local, state_in, gains, params, spread,
        ),
        (
            ((1024, 1024), LOW), (seq, LOW), (seq, LOW), (seq, F32), (lane, F32), (seq, F32),
            ((128, 1024), F32), (seq, F32), ((8, 1024), F32),
        ),
        (((1024, 1024), LOW), ((8, 1024), F32)),
        1,
    )
    pieces = lax.all_to_all(adjoint_local.reshape(slots, 8, 1024), "ctx", 0, 0)
    term_output = column_dot(mixed, grad_out).astype(LOW)
    term_gates = column_dot(act_low, grad_gate).astype(LOW)
    received = core_partner(jnp.where(first, term_output, term_gates))
    (early,) = run(
        early_kernel,
        (jnp.where(first, term_gates, term_output), received),
        (((devices, 8, 1024), LOW),),
    )
    grad_inner, grad_maps, crossings = run(
        inner_kernel,
        (
            spread, value, in_map, out_map, step, decay, fresh, states, grad_ssd, adjoint,
        ),
        ((seq, F32), ((bins, 256), F32), ((bins // Q * 8, 128), F32)),
        (((128, 1024), F32), ((Q, 1024), F32)),
    )
    pieces, grad_inner = lax.optimization_barrier((pieces, grad_inner))
    (carried,) = run(scan_backward, (pieces, decays), (((slots, 8, 1024), F32),))
    adjoint_out = lax.all_to_all(carried, "ctx", 0, 0).reshape(128, 1024)
    adjoint_out, early = lax.optimization_barrier((adjoint_out, early))
    early_got = lax.all_to_all(early, ALL, 0, 0)
    grad_wide, tokens_grad, sums, heads = run(
        grad_kernel,
        (
            tok, row, scale, gains, params, spread, wide, gate_whole, grad_gate, value, in_map,
            step_raw, step, decay, fresh, states, grad_ssd, out_dot, grad_inner, grad_maps,
            crossings, adjoint_out, sums_mix,
        ),
        (((bins, 1408), LOW), (seq, LOW), ((8, 1024), F32), ((8, 128), F32)),
        (((8, 1024), F32),),
    )
    term_wide = column_dot(act_low, grad_wide)
    received = core_partner(
        jnp.where(first, term_wide[:, 640:1280], term_wide[:, :640]).astype(LOW)
    )
    tile = jnp.concatenate(
        [
            jnp.zeros((8, 18), F32),
            heads[:3, :16].reshape(8, 6),
            jnp.zeros((8, 1), F32),
            jnp.broadcast_to(session_ids.astype(F32)[:, None], (8, 1)),
            jnp.zeros((8, 102), F32),
        ],
        axis=1,
    )
    (late,) = run(
        late_kernel,
        (core, term_wide, received, sums, sums_mix, tile),
        (((devices, 8, 768), LOW),),
        (((128, 1024), F32), ((1024, 128), F32)),
        1,
    )
    late_got = lax.all_to_all(late, ALL, 0, 0)
    input_grad, output_grad, totals, table = run(
        functools.partial(sum_kernel, grad_scale),
        (early_got, late_got),
        (((8, 2304), F32), ((8, 1024), F32), ((8, 128), F32), ((8, 128), F32)),
    )
    return (
        tokens_grad[None],
        totals[:, 16],
        input_grad,
        totals[:, :16],
        totals[:, 18:24].reshape(3, 16),
        totals[:, 17],
        output_grad,
        table[:, :sessions].T,
    )


def solution(mesh):
    placed = (
        P("dp", "ctx", None),
        P("dp", "ctx", None),
        P("dp"),
        P(),
        P("dp"),
        P("dp", None),
        P("dp", None),
        P(),
        P("dp"),
        P("dp", None),
    )
    return jax.shard_map(
        per_device,
        mesh=mesh,
        in_specs=placed,
        out_specs=(
            P("dp", "ctx", None),
            P(("dp", "ctx")),
            P(("dp", "ctx"), None),
            P(("dp", "ctx"), None),
            P(),
            P(("dp", "ctx")),
            P(("dp", "ctx"), None),
            P(None, ("dp", "ctx")),
        ),
        check_vma=False,
    )
```

```python
import functools
import math

import jax
import jax.numpy as jnp
from jax import lax
from jax.experimental import pallas as pl
from jax.experimental.pallas import tpu as pltpu
from jax.sharding import PartitionSpec as P

epsilon = 1e-05
ALL = ("dp", "ctx")
Q = 128
F32 = jnp.float32
LOW = jnp.bfloat16
NN = (((1,), (0,)), ((), ()))
NT = (((1,), (1,)), ((), ()))


def dot(a, b, dims=NN):
    return lax.dot_general(a, b, dims, preferred_element_type=F32)


def split(x):
    high = x.astype(LOW)
    return high, (x - high.astype(F32)).astype(LOW)


def dot3(a, b, dims=NN):
    (ah, al), (bh, bl) = split(a), split(b)
    return dot(ah, bh, dims) + dot(ah, bl, dims) + dot(al, bh, dims)


def thirds(x):
    high = x.astype(LOW)
    rest = x - high.astype(F32)
    mid = rest.astype(LOW)
    return high, mid, (rest - mid.astype(F32)).astype(LOW)


def expand(x, spread):
    high = x.astype(LOW).astype(F32)
    rest = x - high
    mid = rest.astype(LOW).astype(F32)
    parts = high + pltpu.roll(mid, 16, 1) + pltpu.roll(rest - mid, 32, 1)
    return dot(parts.astype(LOW), spread)


def by_heads(x, spread):
    high, low = split(x)
    return dot(high, spread, NT) + dot(low, spread, NT)


def of_heads(x):
    return jnp.where(iota(1, x.shape) < 16, x, 0.0)


def select_left(chosen, x):
    high, mid, low = thirds(x)
    return dot(chosen, high) + dot(chosen, mid) + dot(chosen, low)


def sigmoid(x):
    return 1.0 / (1.0 + jnp.exp(-x))


def softplus(x):
    u = jnp.exp(-jnp.abs(x))
    w = 1.0 + u
    log1p = jnp.where(w == 1.0, u, jnp.log(w) * (u / jnp.where(w == 1.0, 1.0, w - 1.0)))
    return jnp.maximum(x, 0.0) + log1p


def iota(dim, shape=(Q, Q)):
    return lax.broadcasted_iota(jnp.int32, shape, dim)


def rows_of(c):
    return pl.ds(pl.multiple_of(c * Q, Q), Q)


def assemble(core, mine, other, whole):
    half = mine.shape[1]
    first = pl.multiple_of(core * half, half)
    second = pl.multiple_of((1 - core) * half, half)
    for i in range(mine.shape[0]):
        whole[pl.ds(2 * half * i + first, half), :] = mine[i]
        whole[pl.ds(2 * half * i + second, half), :] = other[i]


def prep_kernel(
    core_ref, tok, row, mine, other, hp, spread,
    wide, act_low, scale, value, in_map, out_map, step_raw, step, decay, fresh, packed, gains,
    through,
    state, total, rest,
):
    assemble(core_ref[0], mine, other, wide)
    small = wide[:, 1280:1408].astype(F32).T
    gains[0:1, :] = small[16:17, :]
    gains[1:2, :] = small[17:18, :]
    state[...] = jnp.zeros_like(state)
    total[...] = jnp.zeros_like(total)
    ones_low = (iota(0) >= iota(1)).astype(F32).astype(LOW)
    chunks = tok.shape[0] // Q

    def norm(c, carry):
        rows = rows_of(c)
        x = tok[rows, :].astype(F32) + row[0:1, :]
        factor = lax.rsqrt(jnp.mean(x * x, axis=1, keepdims=True) + epsilon)
        act_low[rows, :] = (x * factor * gains[0:1, :]).astype(LOW)
        scale[rows, :] = jnp.broadcast_to(factor, (Q, 128))
        return carry

    lax.fori_loop(0, chunks, norm, 0)
    value[...] = dot(act_low[...], wide[:, :1024])
    rest[...] = dot(act_low[...], wide[:, 1024:1408])

    def body(c, carry):
        rows = rows_of(c)
        value_c = value[rows, :]
        in_c = rest[rows, 0:128]
        in_map[rows, :] = in_c
        out_map[rows, :] = rest[rows, 128:256]
        raw = of_heads(rest[rows, 256:384] + hp[0:1, :])
        step_raw[rows, :] = raw
        size = of_heads(softplus(raw))
        step[rows, :] = size
        logs = select_left(ones_low, -jnp.exp(hp[1:2, :]) * size)
        decay[rows, :] = logs
        last = logs[Q - 1 : Q, :]
        weight = expand(jnp.exp(last - logs) * size, spread[...])
        activated = value_c * sigmoid(value_c)
        fresh_c = dot3(in_c.T, weight * activated)
        fresh[rows, :] = fresh_c
        kept = expand(of_heads(jnp.broadcast_to(jnp.exp(last), (8, 128))), spread[...])
        through[eight(c), :] = kept
        state[...] = kept[0:1, :] * state[...] + fresh_c
        total[...] = total[...] + last
        return carry

    lax.fori_loop(0, chunks, body, 0)
    packed[:, :1024] = state[...]
    packed[:, 1024:1152] = jnp.broadcast_to(jnp.exp(total[0:1, :]), (128, 128))


def scan_forward(pieces, spread, carried, decays):
    count = pieces.shape[0]
    rates = jnp.concatenate([pieces[j, 0:1, 1024:1152] for j in range(count)], axis=0)
    decays[...] = expand(of_heads(rates), spread[...])
    held = jnp.zeros((8, 1024), F32)
    for j in range(count):
        carried[j] = held
        held = decays[j : j + 1, :] * held + pieces[j, :, :1024]


def scan_backward(pieces, decays, carried):
    count = pieces.shape[0]
    held = jnp.zeros((8, 1024), F32)
    for j in range(count - 1, -1, -1):
        carried[j] = held
        held = decays[j : j + 1, :] * held + pieces[j]


def pair_gaps(logs, logs_t, pair, transposed):
    gaps = []
    for head in (2 * pair, 2 * pair + 1):
        column = jnp.broadcast_to(logs[:, head : head + 1], (Q, Q))
        across = jnp.broadcast_to(logs_t[head : head + 1, :], (Q, Q))
        if transposed:
            gap = jnp.where(iota(1) >= iota(0), across - column, -1e30)
        else:
            gap = jnp.where(iota(0) >= iota(1), column - across, -1e30)
        gaps.append(jnp.exp(gap))
    return gaps


def by_head(x, axis):
    first = iota(1) < 64
    return jnp.concatenate([jnp.where(first, x, 0.0), jnp.where(first, 0.0, x)], axis=axis)


def widen(row, spread):
    return expand(jnp.broadcast_to(row, (8, 128)), spread)[0:1, :]


def eight(c):
    return pl.ds(pl.multiple_of(8 * c, 8), 8)


def local_kernel(value, in_map, out_map, step, decay, fresh, through, spread, y_local, states, ssd, scaled, held):
    held[...] = jnp.zeros_like(held)

    def body(c, carry):
        rows = rows_of(c)
        states[rows, :] = held[...]
        logs = decay[rows, :]
        logs_t = logs.T
        value_c = value[rows, :]
        scaled[...] = expand(step[rows, :], spread[...]) * (value_c * sigmoid(value_c))
        reach = expand(of_heads(jnp.exp(logs)), spread[...])
        out_c = out_map[rows, :]
        scores = dot3(out_c, in_map[rows, :], NT)
        for pair in range(8):
            lanes = slice(128 * pair, 128 * pair + 128)
            one, two = pair_gaps(logs, logs_t, pair, False)
            weighted = jnp.concatenate([one * scores, two * scores], axis=1)
            ssd[:, lanes] = dot3(weighted, by_head(scaled[:, lanes], 0))
        y_local[rows, :] = ssd[...] + reach * dot3(out_c, held[...])
        held[...] = through[eight(c), :][0:1, :] * held[...] + fresh[rows, :]
        return carry

    lax.fori_loop(0, value.shape[0] // Q, body, 0)


def gate_kernel(
    place_ref, act_low, mine, other, grad_out, gate_whole, gate, grad_mixed, out_whole
):
    core, group = place_ref[0], place_ref[1]
    half = mine.shape[1]
    for i in range(mine.shape[0]):
        start = ((group + i // 2) % 4 * 2 + i % 2) * (2 * half)
        for block, turn in ((mine, core), (other, 1 - core)):
            rows = pl.ds(pl.multiple_of(start + turn * half, half), half)
            gate_whole[rows, :] = block[i, :, :1024]
            out_whole[rows, :] = block[i, :, 1024:]
    gate[...] = dot(act_low[...], gate_whole[...])
    grad_mixed[...] = dot(grad_out[...], out_whole[...], NT)


def mix_kernel(
    gate_all, grad_mixed_all, value, out_map, decay, y_local, states_local, state_in, gains, hp,
    through, spread,
    mixed, grad_gate, grad_ssd, out_dot, adjoint, adjoint_local, states, sums,
    base,
):
    base[...] = jnp.ones_like(base)
    adjoint_local[...] = jnp.zeros_like(adjoint_local)
    sums[...] = jnp.zeros_like(sums)
    skip = widen(hp[2:3, :], spread[...])

    def body(c, carry):
        rows = rows_of(c)
        before = base[0:1, :]
        entering = before * state_in[...]
        states[rows, :] = states_local[rows, :] + entering
        logs = decay[rows, :]
        value_c = value[rows, :]
        activated = value_c * sigmoid(value_c)
        reach = expand(of_heads(jnp.exp(logs)), spread[...])
        out_c = out_map[rows, :]
        y_state = y_local[rows, :] + reach * dot3(out_c, entering)
        y = y_state + skip * activated
        gate = gate_all[rows, :]
        grad_mixed = grad_mixed_all[rows, :]
        sig = sigmoid(gate)
        silu = gate * sig
        gated = y * silu
        gate_scale = lax.rsqrt(jnp.mean(gated * gated, axis=1, keepdims=True) + epsilon)
        gnorm = gated * gate_scale
        mixed[rows, :] = (gnorm * gains[1:2, :]).astype(LOW)
        along = grad_mixed * gnorm
        sums[0:1, :] = sums[0:1, :] + jnp.sum(along, axis=0, keepdims=True)
        grad_gnorm = grad_mixed * gains[1:2, :]
        mean = jnp.mean(grad_gnorm * gnorm, axis=1, keepdims=True)
        grad_gated = gate_scale * (grad_gnorm - gnorm * mean)
        grad_gate[rows, :] = (grad_gated * y * sig * (1.0 + gate * (1.0 - sig))).astype(LOW)
        grad_y = grad_gated * silu
        grad_ssd[rows, :] = grad_y
        sums[1:2, :] = sums[1:2, :] + jnp.sum(grad_y * activated, axis=0, keepdims=True)
        out_dot[rows, :] = by_heads(grad_y * y_state, spread[...])
        adjoint_c = dot3(out_c.T, reach * grad_y)
        adjoint[rows, :] = adjoint_c
        adjoint_local[...] = adjoint_local[...] + before * adjoint_c
        base[0:1, :] = before * through[eight(c), :][0:1, :]
        return carry

    lax.fori_loop(0, value.shape[0] // Q, body, 0)


def inner_kernel(
    spread, value, in_map, out_map, step, decay, fresh, through_all, states, grad_ssd, adjoint,
    grad_scaled, grad_maps, crossings,
    held, scaled,
):
    held[...] = jnp.zeros_like(held)
    chunks = value.shape[0] // Q

    def body(i, carry):
        c = chunks - 1 - i
        rows = rows_of(c)
        logs = decay[rows, :]
        logs_t = logs.T
        last = logs[Q - 1 : Q, :]
        in_c = in_map[rows, :]
        out_c = out_map[rows, :]
        through = through_all[eight(c), :][0:1, :]
        state_end = through * states[rows, :] + fresh[rows, :]
        crossing = jnp.sum(held[...] * state_end, axis=0, keepdims=True)
        crossing = by_heads(jnp.broadcast_to(crossing, (8, 1024)), spread[...])
        crossings[eight(c), :] = crossing
        value_c = value[rows, :]
        scaled[...] = expand(step[rows, :], spread[...]) * (value_c * sigmoid(value_c))
        tail = expand(of_heads(jnp.exp(last - logs)), spread[...])
        grad_scaled[rows, :] = tail * dot3(in_c, held[...])
        grad_in = dot3(tail * scaled[...], held[...], NT)
        reach = expand(of_heads(jnp.exp(logs)), spread[...])
        grad_out_map = dot3(reach * grad_ssd[rows, :], states[rows, :], NT)
        scores = dot3(in_c, out_c, NT)
        grad_scores = jnp.zeros((Q, Q), F32)
        for pair in range(8):
            lanes = slice(128 * pair, 128 * pair + 128)
            one, two = pair_gaps(logs, logs_t, pair, True)
            grad_pair = by_head(grad_ssd[rows, lanes], 0)
            weighted = jnp.concatenate([one * scores, two * scores], axis=1)
            grad_scaled[rows, lanes] = grad_scaled[rows, lanes] + dot3(weighted, grad_pair)
            both = dot3(scaled[:, lanes], grad_pair, NT)
            grad_scores = grad_scores + one * both[:, :Q] + two * both[:, Q:]
        grad_maps[rows, 0:128] = grad_in + dot3(grad_scores, out_c)
        grad_maps[rows, 128:256] = grad_out_map + dot3(grad_scores.T, in_c)
        held[...] = adjoint[rows, :] + through * held[...]
        return carry

    lax.fori_loop(0, chunks, body, 0)


def grad_kernel(
    tok, row, scale, gains, hp, spread, wide, gate_whole, grad_gate, value, in_map,
    step_raw, step, decay, fresh, through_all, states, grad_ssd, out_dot, grad_inner, grad_maps,
    crossings, adjoint_out, sums_mix,
    grad_wide, grad_steps, tokens_grad, sums, heads,
    after, grad_act_all,
):
    after[...] = jnp.ones_like(after)
    sums[...] = jnp.zeros_like(sums)
    heads[...] = jnp.zeros_like(heads)
    heads[2:3, :] = by_heads(sums_mix[...], spread[...])[1:2, :]
    skip = widen(hp[2:3, :], spread[...])
    chunks = tok.shape[0] // Q
    ones_up = (iota(1) >= iota(0)).astype(F32).astype(LOW)

    def body(i, carry):
        c = chunks - 1 - i
        rows = rows_of(c)
        logs = decay[rows, :]
        last = logs[Q - 1 : Q, :]
        size = step[rows, :]
        through = through_all[eight(c), :][0:1, :]
        leaving = after[0:1, :] * adjoint_out[...]
        state_end = through * states[rows, :] + fresh[rows, :]
        crossing = jnp.sum(leaving * state_end, axis=0, keepdims=True)
        crossing = by_heads(jnp.broadcast_to(crossing, (8, 1024)), spread[...])
        crossing = (crossing + crossings[eight(c), :])[0:1, :]
        value_c = value[rows, :]
        sig = sigmoid(value_c)
        activated = value_c * sig
        size_wide = expand(size, spread[...])
        tail = expand(of_heads(jnp.exp(last - logs)), spread[...])
        grad_scaled = grad_inner[rows, :] + tail * dot3(in_map[rows, :], leaving)
        grad_in = grad_maps[rows, 0:128] + dot3(tail * (size_wide * activated), leaving, NT)
        per_step = by_heads(activated * grad_scaled, spread[...])
        grad_logs = out_dot[rows, :] - size * per_step
        grad_rate = select_left(ones_up, grad_logs) + crossing
        speed = jnp.exp(hp[1:2, :])
        raw = step_raw[rows, :]
        grad_raw = jnp.where(iota(1) < 16, (per_step - speed * grad_rate) * sigmoid(raw), 0.0)
        heads[0:1, :] = heads[0:1, :] + jnp.sum(grad_raw, axis=0, keepdims=True)
        heads[1:2, :] = heads[1:2, :] - jnp.sum(
            grad_rate * (speed * size), axis=0, keepdims=True
        )
        grad_act_c = size_wide * grad_scaled + skip * grad_ssd[rows, :]
        grad_wide[rows, 0:1024] = (grad_act_c * sig * (1.0 + value_c * (1.0 - sig))).astype(LOW)
        grad_wide[rows, 1024:1152] = grad_in.astype(LOW)
        grad_wide[rows, 1152:1280] = grad_maps[rows, 128:256].astype(LOW)
        grad_steps[rows, :] = grad_raw.astype(LOW)
        after[0:1, :] = after[0:1, :] * through
        return carry

    lax.fori_loop(0, chunks, body, 0)
    grad_act_all[...] = (
        dot(grad_wide[...], wide[:, :1280], NT)
        + dot(grad_steps[...], wide[:, 1280:1408], NT)
        + dot(grad_gate[...], gate_whole[...], NT)
    )

    def finish(c, carry):
        rows = rows_of(c)
        grad_act = grad_act_all[rows, :]
        factor = scale[rows, 0:1]
        normed = (tok[rows, :].astype(F32) + row[0:1, :]) * factor
        sums[0:1, :] = sums[0:1, :] + jnp.sum(grad_act * normed, axis=0, keepdims=True)
        grad_normed = grad_act * gains[0:1, :]
        mean = jnp.mean(grad_normed * normed, axis=1, keepdims=True)
        grad_input = factor * (grad_normed - normed * mean)
        tokens_grad[rows, :] = grad_input.astype(LOW)
        sums[1:2, :] = sums[1:2, :] + jnp.sum(grad_input, axis=0, keepdims=True)
        return carry

    lax.fori_loop(0, chunks, finish, 0)


def early_kernel(mine, other, packed):
    def body(j, carry):
        rows = pl.ds(pl.multiple_of(j * Q, Q), Q)
        both = mine[rows, :].astype(F32) + other[rows, :].astype(F32)
        packed[pl.ds(j * 16, 16)] = both.reshape(16, 8, -1).astype(LOW)
        return carry

    lax.fori_loop(0, mine.shape[0] // Q, body, 0)


def late_kernel(core_ref, term, steps, other, sums, sums_mix, tile, packed, across, columns):
    across[...] = jnp.zeros_like(across)
    across[16:17, :] = sums[0:1, :]
    across[17:18, :] = sums_mix[0:1, :]
    across[24:25, :] = sums[1:2, :]
    columns[...] = across[...].T
    first = core_ref[0] == 0
    lane = iota(1)

    def body(j, carry):
        rows = pl.ds(pl.multiple_of(j * Q, Q), Q)
        low, high = term[rows, 0:640].astype(F32), term[rows, 640:1280].astype(F32)
        mine = jnp.where(first, low, high)
        both = mine.astype(F32) + other[rows, :].astype(F32)
        packed[pl.ds(j * 16, 16), :, 0:640] = both.reshape(16, 8, 640).astype(LOW)
        extra = (steps[rows, :] + columns[rows, :]).reshape(16, 8, 128)
        extra = (extra + tile[...][None]).reshape(Q, 128)
        coarse = extra.astype(LOW).astype(F32)
        fine = pltpu.roll(extra - coarse, 64, 1)
        small = jnp.where(lane < 64, coarse, fine)
        packed[pl.ds(j * 16, 16), :, 640:768] = small.reshape(16, 8, 128).astype(LOW)
        return carry

    lax.fori_loop(0, term.shape[0] // Q, body, 0)


def early_sum(early, gates, outs):
    gates[...] = jnp.zeros_like(gates)
    outs[...] = jnp.zeros_like(outs)

    def body(j, carry):
        gates[...] += early[2 * j].astype(F32)
        outs[...] += early[2 * j + 1].astype(F32)
        return carry

    lax.fori_loop(0, early.shape[0] // 2, body, 0, unroll=4)


def late_sum(grad_scale, late, gates, outs, input_grad, output_grad, small, table):
    input_grad[...] = jnp.zeros_like(input_grad)
    small[...] = jnp.zeros_like(small)
    table[...] = jnp.zeros_like(table)
    input_grad[:, 0:1024] = gates[...] * grad_scale
    output_grad[...] = outs[...] * grad_scale
    lane = iota(1, (8, 128)).astype(F32)

    def body(j, carry):
        input_grad[:, 1024:1664] += late[2 * j, :, 0:640].astype(F32)
        input_grad[:, 1664:2304] += late[2 * j + 1, :, 0:640].astype(F32)
        for k in range(2):
            parts = late[2 * j + k, :, 640:768].astype(F32)
            parts = parts + pltpu.roll(parts, 64, 1)
            small[...] += parts
            table[...] += jnp.where(lane == parts[:, 25:26], parts[:, 24:25], 0.0)
        return carry

    lax.fori_loop(0, late.shape[0] // 2, body, 0, unroll=4)
    input_grad[:, 1024:2304] = input_grad[:, 1024:2304] * grad_scale
    small[...] = small[...] * grad_scale
    table[...] = table[...] * grad_scale


def at_origin(rank, *unused):
    return (0,) * rank


def run(kernel, args, outs, scratch=(), scalars=0):
    specs = [
        pl.BlockSpec(
            arg.shape, functools.partial(at_origin, arg.ndim), pipeline_mode=pl.Buffered(1)
        )
        for arg in args[scalars:]
    ]
    out_specs = [
        pl.BlockSpec(shape, functools.partial(at_origin, len(shape)), pipeline_mode=pl.Buffered(1))
        for shape, _ in outs
    ]
    return pl.pallas_call(
        kernel,
        name=getattr(kernel, "__name__", "late_sum"),
        out_shape=[jax.ShapeDtypeStruct(shape, dtype) for shape, dtype in outs],
        grid_spec=pltpu.PrefetchScalarGridSpec(
            num_scalar_prefetch=scalars,
            grid=(1,),
            in_specs=specs,
            out_specs=out_specs,
            scratch_shapes=[pltpu.VMEM(shape, dtype) for shape, dtype in scratch],
        ),
        compiler_params=pltpu.CompilerParams(vmem_limit_bytes=60 << 20),
    )(*args)


def core_partner(value):
    flips = [(i, i ^ 1) for i in range(lax.axis_size("dp") * lax.axis_size("ctx"))]
    return lax.ppermute(value, ALL, flips)


def on_first_core():
    return lax.axis_index("ctx") % 2 == 0


def gather_rows(shard):
    half = shard.shape[0] // 2
    count = lax.axis_size("dp")
    mine = jnp.where(on_first_core(), shard[:half], shard[half:])
    pieces = lax.all_to_all(jnp.broadcast_to(mine[None], (count,) + mine.shape), "dp", 0, 0)
    return pieces, core_partner(pieces)


def moved(value, to):
    count = lax.axis_size("dp") * lax.axis_size("ctx")
    return lax.ppermute(value, ALL, [(i, to(i) % count) for i in range(count)])


def ring_near(mine):
    slots = lax.axis_size("ctx")
    return moved(mine, lambda i: i ^ slots)


def ring_sides(mine, near):
    step = 2 * lax.axis_size("ctx")
    even = lax.axis_index("dp") % 2 == 0
    pair = jnp.stack([jnp.where(even, mine, near), jnp.where(even, near, mine)])
    return pair, moved(pair, lambda i: i + step), moved(pair, lambda i: i - step)


def ring_far(lower, upper):
    step = 2 * lax.axis_size("ctx")
    half = lower.shape[1] // 2
    far_low = moved(lower[:, :half], lambda i: i + step)
    far_high = moved(upper[:, half:], lambda i: i - step)
    return far_low, far_high


def column_dot(a, b):
    return lax.dot_general(a, b, (((0,), (0,)), ((), ())), preferred_element_type=F32)


def per_device(
    tokens,
    grad_output,
    session_ids,
    session_table,
    norm_gain,
    input_weight,
    step_weight,
    head_params,
    gate_gain,
    output_weight,
):
    tok, grad_out = tokens[0], grad_output[0]
    bins = tok.shape[0]
    devices = lax.axis_size("dp") * lax.axis_size("ctx")
    slots = lax.axis_size("ctx")
    sessions = session_table.shape[0]
    grad_scale = 1.0 / math.sqrt(bins * devices)
    core = (lax.axis_index("ctx") % 2).astype(jnp.int32)[None]
    first = on_first_core()
    row = lax.dynamic_slice(session_table, (session_ids[0], 0), (1, 1024)).astype(F32)
    row = jnp.broadcast_to(row, (8, 1024))
    params = jnp.pad(head_params, ((0, 5), (0, 112)))
    copies = jnp.arange(128)[:, None]
    spread = ((jnp.arange(1024)[None, :] // 64 == copies % 16) & (copies < 48)).astype(LOW)
    shard = jnp.concatenate(
        [
            input_weight[:, 1024:],
            step_weight,
            norm_gain[:, None],
            gate_gain[:, None],
            jnp.zeros((input_weight.shape[0], 110), LOW),
        ],
        axis=1,
    )
    mine, other = gather_rows(shard)
    rest = jnp.concatenate([input_weight[:, :1024], output_weight], axis=1)
    rest_half = jnp.where(first, rest[:64], rest[64:])
    mine, rest_half = lax.optimization_barrier((mine, rest_half))
    near = ring_near(rest_half)
    place = jnp.stack([core[0], lax.axis_index("dp").astype(jnp.int32) // 2])
    seq = (bins, 1024)
    lane = (bins, 128)
    prepared = run(
        prep_kernel,
        (core, tok, row, mine, other, params, spread),
        (
            ((1024, 1408), LOW), (seq, LOW), (lane, F32), (seq, F32), (lane, F32), (lane, F32),
            (lane, F32), (lane, F32), (lane, F32), (seq, F32), ((128, 1152), F32), ((8, 1024), F32),
            ((bins // Q * 8, 1024), F32),
        ),
        (((128, 1024), F32), ((8, 128), F32), ((bins, 384), F32)),
        1,
    )
    wide, act_low, scale, value, in_map, out_map, step_raw, step = prepared[:8]
    decay, fresh, packed, gains, through = prepared[8:]
    near, packed = lax.optimization_barrier((near, packed))
    pair, lower, upper = ring_sides(rest_half, near)
    pieces = lax.all_to_all(packed.reshape(slots, 8, 1152), "ctx", 0, 0)
    y_local, states_local = run(
        local_kernel,
        (value, in_map, out_map, step, decay, fresh, through, spread),
        ((seq, F32), (seq, F32)),
        (((Q, 1024), F32), ((Q, 1024), F32), ((128, 1024), F32)),
    )
    pieces, y_local, lower, upper = lax.optimization_barrier((pieces, y_local, lower, upper))
    far_low, far_high = ring_far(lower, upper)
    carried, decays = run(
        scan_forward, (pieces, spread), (((slots, 8, 1024), F32), ((slots, 1024), F32))
    )
    carried, far_low, far_high = lax.optimization_barrier((carried, far_low, far_high))
    far = jnp.concatenate([far_low, far_high], axis=1)
    rest_mine = jnp.concatenate([pair, upper, far, lower], axis=0)
    rest_other = core_partner(rest_mine)
    state_in = lax.all_to_all(carried, "ctx", 0, 0).reshape(128, 1024)
    gate_whole, gate, grad_mixed = run(
        gate_kernel,
        (place, act_low, rest_mine, rest_other, grad_out),
        (((1024, 1024), LOW), (seq, F32), (seq, F32)),
        (((1024, 1024), LOW),),
        1,
    )
    mixed, grad_gate, grad_ssd, out_dot, adjoint, adjoint_local, states, sums_mix = run(
        mix_kernel,
        (
            gate, grad_mixed, value, out_map, decay, y_local, states_local, state_in, gains,
            params, through, spread,
        ),
        (
            (seq, LOW), (seq, LOW), (seq, F32), (lane, F32), (seq, F32), ((128, 1024), F32),
            (seq, F32), ((8, 1024), F32),
        ),
        (((8, 1024), F32),),
    )
    pieces = lax.all_to_all(adjoint_local.reshape(slots, 8, 1024), "ctx", 0, 0)
    grad_inner, grad_maps, crossings = run(
        inner_kernel,
        (
            spread, value, in_map, out_map, step, decay, fresh, through, states, grad_ssd,
            adjoint,
        ),
        ((seq, F32), ((bins, 256), F32), ((bins // Q * 8, 128), F32)),
        (((128, 1024), F32), ((Q, 1024), F32)),
    )
    pieces, grad_inner = lax.optimization_barrier((pieces, grad_inner))
    (carried,) = run(scan_backward, (pieces, decays), (((slots, 8, 1024), F32),))
    carried, mixed, early_gate = lax.optimization_barrier((carried, mixed, grad_gate))
    term_output = column_dot(mixed, grad_out).astype(LOW)
    term_gates = column_dot(act_low, early_gate).astype(LOW)
    received = core_partner(jnp.where(first, term_output, term_gates))
    (early,) = run(
        early_kernel,
        (jnp.where(first, term_gates, term_output), received),
        (((devices, 8, 1024), LOW),),
    )
    adjoint_out = lax.all_to_all(carried, "ctx", 0, 0).reshape(128, 1024)
    adjoint_out, early = lax.optimization_barrier((adjoint_out, early))
    early_got = lax.all_to_all(early, ALL, 0, 0)
    grad_wide, grad_steps, tokens_grad, sums, heads = run(
        grad_kernel,
        (
            tok, row, scale, gains, params, spread, wide, gate_whole, grad_gate, value, in_map,
            step_raw, step, decay, fresh, through, states, grad_ssd, out_dot, grad_inner,
            grad_maps, crossings, adjoint_out, sums_mix,
        ),
        (
            ((bins, 1280), LOW), (lane, LOW), (seq, LOW), ((8, 1024), F32), ((8, 128), F32),
        ),
        (((8, 1024), F32), (seq, F32)),
    )
    term_low = column_dot(act_low, grad_wide).astype(LOW)
    term_steps = column_dot(act_low, grad_steps)
    received = core_partner(jnp.where(first, term_low[:, 640:], term_low[:, :640]))
    tile = jnp.concatenate(
        [
            jnp.zeros((8, 18), F32),
            heads[:3, :16].reshape(8, 6),
            jnp.zeros((8, 1), F32),
            jnp.broadcast_to(session_ids.astype(F32)[:, None], (8, 1)),
            jnp.zeros((8, 102), F32),
        ],
        axis=1,
    )
    (late,) = run(
        late_kernel,
        (core, term_low, term_steps, received, sums, sums_mix, tile),
        (((devices, 8, 768), LOW),),
        (((128, 1024), F32), ((1024, 128), F32)),
        1,
    )
    late_got = lax.all_to_all(late, ALL, 0, 0)
    gates, outs = run(early_sum, (early_got,), (((8, 1024), F32), ((8, 1024), F32)))
    input_grad, output_grad, totals, table = run(
        functools.partial(late_sum, grad_scale),
        (late_got, gates, outs),
        (((8, 2304), F32), ((8, 1024), F32), ((8, 128), F32), ((8, 128), F32)),
    )
    return (
        tokens_grad[None],
        totals[:, 16],
        input_grad,
        totals[:, :16],
        totals[:, 18:24].reshape(3, 16),
        totals[:, 17],
        output_grad,
        table[:, :sessions].T,
    )


def solution(mesh):
    placed = (
        P("dp", "ctx", None),
        P("dp", "ctx", None),
        P("dp"),
        P(),
        P("dp"),
        P("dp", None),
        P("dp", None),
        P(),
        P("dp"),
        P("dp", None),
    )
    return jax.shard_map(
        per_device,
        mesh=mesh,
        in_specs=placed,
        out_specs=(
            P("dp", "ctx", None),
            P(("dp", "ctx")),
            P(("dp", "ctx"), None),
            P(("dp", "ctx"), None),
            P(),
            P(("dp", "ctx")),
            P(("dp", "ctx"), None),
            P(None, ("dp", "ctx")),
        ),
        check_vma=False,
    )
```

```python
import functools
import math

import jax
import jax.numpy as jnp
from jax import lax
from jax.experimental import pallas as pl
from jax.experimental.pallas import tpu as pltpu
from jax.sharding import PartitionSpec as P

epsilon = 1e-05
ALL = ("dp", "ctx")
Q = 128
F32 = jnp.float32
LOW = jnp.bfloat16
NN = (((1,), (0,)), ((), ()))
NT = (((1,), (1,)), ((), ()))


def dot(a, b, dims=NN):
    return lax.dot_general(a, b, dims, preferred_element_type=F32)


def split(x):
    high = x.astype(LOW)
    return high, (x - high.astype(F32)).astype(LOW)


def dot3(a, b, dims=NN):
    (ah, al), (bh, bl) = split(a), split(b)
    return dot(ah, bh, dims) + dot(ah, bl, dims) + dot(al, bh, dims)


def thirds(x):
    high = x.astype(LOW)
    rest = x - high.astype(F32)
    mid = rest.astype(LOW)
    return high, mid, (rest - mid.astype(F32)).astype(LOW)


def expand(x, spread):
    high = x.astype(LOW).astype(F32)
    rest = x - high
    mid = rest.astype(LOW).astype(F32)
    parts = high + pltpu.roll(mid, 16, 1) + pltpu.roll(rest - mid, 32, 1)
    return dot(parts.astype(LOW), spread)


def by_heads(x, spread):
    high, low = split(x)
    return dot(high, spread, NT) + dot(low, spread, NT)


def of_heads(x):
    return jnp.where(iota(1, x.shape) < 16, x, 0.0)


def select_left(chosen, x):
    high, mid, low = thirds(x)
    return dot(chosen, high) + dot(chosen, mid) + dot(chosen, low)


def sigmoid(x):
    return 1.0 / (1.0 + jnp.exp(-x))


def softplus(x):
    u = jnp.exp(-jnp.abs(x))
    w = 1.0 + u
    log1p = jnp.where(w == 1.0, u, jnp.log(w) * (u / jnp.where(w == 1.0, 1.0, w - 1.0)))
    return jnp.maximum(x, 0.0) + log1p


def iota(dim, shape=(Q, Q)):
    return lax.broadcasted_iota(jnp.int32, shape, dim)


def rows_of(c):
    return pl.ds(pl.multiple_of(c * Q, Q), Q)


def assemble(core, mine, other, whole):
    half = mine.shape[1]
    first = pl.multiple_of(core * half, half)
    second = pl.multiple_of((1 - core) * half, half)
    for i in range(mine.shape[0]):
        whole[pl.ds(2 * half * i + first, half), :] = mine[i]
        whole[pl.ds(2 * half * i + second, half), :] = other[i]


def prep_kernel(
    core_ref, tok, row, mine, other, hp, spread,
    wide, act_low, scale, value, in_map, out_map, step_raw, step, decay, fresh, packed, gains,
    through,
    state, total, rest,
):
    assemble(core_ref[0], mine, other, wide)
    small = wide[:, 1280:1408].astype(F32).T
    gains[0:1, :] = small[16:17, :]
    gains[1:2, :] = small[17:18, :]
    state[...] = jnp.zeros_like(state)
    total[...] = jnp.zeros_like(total)
    ones_low = (iota(0) >= iota(1)).astype(F32).astype(LOW)
    chunks = tok.shape[0] // Q

    def norm(c, carry):
        rows = rows_of(c)
        x = tok[rows, :].astype(F32) + row[0:1, :]
        factor = lax.rsqrt(jnp.mean(x * x, axis=1, keepdims=True) + epsilon)
        act_low[rows, :] = (x * factor * gains[0:1, :]).astype(LOW)
        scale[rows, :] = jnp.broadcast_to(factor, (Q, 128))
        return carry

    lax.fori_loop(0, chunks, norm, 0)
    value[...] = dot(act_low[...], wide[:, :1024])
    rest[...] = dot(act_low[...], wide[:, 1024:1408])

    def body(c, carry):
        rows = rows_of(c)
        value_c = value[rows, :]
        in_c = rest[rows, 0:128]
        in_map[rows, :] = in_c
        out_map[rows, :] = rest[rows, 128:256]
        raw = of_heads(rest[rows, 256:384] + hp[0:1, :])
        step_raw[rows, :] = raw
        size = of_heads(softplus(raw))
        step[rows, :] = size
        logs = select_left(ones_low, -jnp.exp(hp[1:2, :]) * size)
        decay[rows, :] = logs
        last = logs[Q - 1 : Q, :]
        weight = expand(jnp.exp(last - logs) * size, spread[...])
        activated = value_c * sigmoid(value_c)
        fresh_c = dot3(in_c.T, weight * activated)
        fresh[rows, :] = fresh_c
        kept = expand(of_heads(jnp.broadcast_to(jnp.exp(last), (8, 128))), spread[...])
        through[eight(c), :] = kept
        state[...] = kept[0:1, :] * state[...] + fresh_c
        total[...] = total[...] + last
        return carry

    lax.fori_loop(0, chunks, body, 0)
    packed[:, :1024] = state[...]
    packed[:, 1024:1152] = jnp.broadcast_to(jnp.exp(total[0:1, :]), (128, 128))


def scan_forward(pieces, spread, carried, decays):
    count = pieces.shape[0]
    rates = jnp.concatenate([pieces[j, 0:1, 1024:1152] for j in range(count)], axis=0)
    decays[...] = expand(of_heads(rates), spread[...])
    held = jnp.zeros((8, 1024), F32)
    for j in range(count):
        carried[j] = held
        held = decays[j : j + 1, :] * held + pieces[j, :, :1024]


def scan_backward(pieces, decays, carried):
    count = pieces.shape[0]
    held = jnp.zeros((8, 1024), F32)
    for j in range(count - 1, -1, -1):
        carried[j] = held
        held = decays[j : j + 1, :] * held + pieces[j]


def pair_gaps(logs, logs_t, pair, transposed):
    gaps = []
    for head in (2 * pair, 2 * pair + 1):
        column = jnp.broadcast_to(logs[:, head : head + 1], (Q, Q))
        across = jnp.broadcast_to(logs_t[head : head + 1, :], (Q, Q))
        if transposed:
            gap = jnp.where(iota(1) >= iota(0), across - column, -1e30)
        else:
            gap = jnp.where(iota(0) >= iota(1), column - across, -1e30)
        gaps.append(jnp.exp(gap))
    return gaps


def by_head(x, axis):
    first = iota(1) < 64
    return jnp.concatenate([jnp.where(first, x, 0.0), jnp.where(first, 0.0, x)], axis=axis)


def widen(row, spread):
    return expand(jnp.broadcast_to(row, (8, 128)), spread)[0:1, :]


def eight(c):
    return pl.ds(pl.multiple_of(8 * c, 8), 8)


def local_kernel(value, in_map, out_map, step, decay, fresh, through, spread, y_local, states, ssd, scaled, held):
    @pl.when(pl.program_id(0) == 0)
    def start():
        held[...] = jnp.zeros_like(held)

    def body(c, carry):
        rows = slice(None)
        states[rows, :] = held[...]
        logs = decay[rows, :]
        logs_t = logs.T
        value_c = value[rows, :]
        scaled[...] = expand(step[rows, :], spread[...]) * (value_c * sigmoid(value_c))
        reach = expand(of_heads(jnp.exp(logs)), spread[...])
        out_c = out_map[rows, :]
        scores = dot3(out_c, in_map[rows, :], NT)
        for pair in range(8):
            lanes = slice(128 * pair, 128 * pair + 128)
            one, two = pair_gaps(logs, logs_t, pair, False)
            weighted = jnp.concatenate([one * scores, two * scores], axis=1)
            ssd[:, lanes] = dot3(weighted, by_head(scaled[:, lanes], 0))
        y_local[rows, :] = ssd[...] + reach * dot3(out_c, held[...])
        held[...] = through[eight(c), :][0:1, :] * held[...] + fresh[rows, :]
        return carry

    body(pl.program_id(0), 0)


def gate_kernel(
    place_ref, act_low, mine, other, grad_out, gate_whole, gate, grad_mixed, out_whole
):
    core, group = place_ref[0], place_ref[1]
    half = mine.shape[1]
    for i in range(mine.shape[0]):
        start = ((group + i // 2) % 4 * 2 + i % 2) * (2 * half)
        for block, turn in ((mine, core), (other, 1 - core)):
            rows = pl.ds(pl.multiple_of(start + turn * half, half), half)
            gate_whole[rows, :] = block[i, :, :1024]
            out_whole[rows, :] = block[i, :, 1024:]
    gate[...] = dot(act_low[...], gate_whole[...])
    grad_mixed[...] = dot(grad_out[...], out_whole[...], NT)


def mix_kernel(
    gate_all, grad_mixed_all, value, out_map, decay, y_local, states_local, state_in, gains, hp,
    through, spread,
    mixed, grad_gate, grad_ssd, out_dot, adjoint, adjoint_local, states, sums,
    base,
):
    @pl.when(pl.program_id(0) == 0)
    def start():
        base[...] = jnp.ones_like(base)
        adjoint_local[...] = jnp.zeros_like(adjoint_local)
        sums[...] = jnp.zeros_like(sums)

    skip = widen(hp[2:3, :], spread[...])

    def body(c, carry):
        rows = slice(None)
        before = base[0:1, :]
        entering = before * state_in[...]
        states[rows, :] = states_local[rows, :] + entering
        logs = decay[rows, :]
        value_c = value[rows, :]
        activated = value_c * sigmoid(value_c)
        reach = expand(of_heads(jnp.exp(logs)), spread[...])
        out_c = out_map[rows, :]
        y_state = y_local[rows, :] + reach * dot3(out_c, entering)
        y = y_state + skip * activated
        gate = gate_all[rows, :]
        grad_mixed = grad_mixed_all[rows, :]
        sig = sigmoid(gate)
        silu = gate * sig
        gated = y * silu
        gate_scale = lax.rsqrt(jnp.mean(gated * gated, axis=1, keepdims=True) + epsilon)
        gnorm = gated * gate_scale
        mixed[rows, :] = (gnorm * gains[1:2, :]).astype(LOW)
        along = grad_mixed * gnorm
        sums[0:1, :] = sums[0:1, :] + jnp.sum(along, axis=0, keepdims=True)
        grad_gnorm = grad_mixed * gains[1:2, :]
        mean = jnp.mean(grad_gnorm * gnorm, axis=1, keepdims=True)
        grad_gated = gate_scale * (grad_gnorm - gnorm * mean)
        grad_gate[rows, :] = (grad_gated * y * sig * (1.0 + gate * (1.0 - sig))).astype(LOW)
        grad_y = grad_gated * silu
        grad_ssd[rows, :] = grad_y
        sums[1:2, :] = sums[1:2, :] + jnp.sum(grad_y * activated, axis=0, keepdims=True)
        out_dot[rows, :] = by_heads(grad_y * y_state, spread[...])
        adjoint_c = dot3(out_c.T, reach * grad_y)
        adjoint[rows, :] = adjoint_c
        adjoint_local[...] = adjoint_local[...] + before * adjoint_c
        base[0:1, :] = before * through[eight(c), :][0:1, :]
        return carry

    body(pl.program_id(0), 0)


def inner_kernel(
    spread, value, in_map, out_map, step, decay, fresh, through_all, states, grad_ssd, adjoint,
    grad_scaled, grad_maps, crossings,
    held, scaled,
):
    chunks = pl.num_programs(0)

    @pl.when(pl.program_id(0) == 0)
    def start():
        held[...] = jnp.zeros_like(held)

    def body(i, carry):
        c = chunks - 1 - i
        rows = slice(None)
        logs = decay[rows, :]
        logs_t = logs.T
        last = logs[Q - 1 : Q, :]
        in_c = in_map[rows, :]
        out_c = out_map[rows, :]
        through = through_all[eight(c), :][0:1, :]
        state_end = through * states[rows, :] + fresh[rows, :]
        crossing = jnp.sum(held[...] * state_end, axis=0, keepdims=True)
        crossing = by_heads(jnp.broadcast_to(crossing, (8, 1024)), spread[...])
        crossings[eight(c), :] = crossing
        value_c = value[rows, :]
        scaled[...] = expand(step[rows, :], spread[...]) * (value_c * sigmoid(value_c))
        tail = expand(of_heads(jnp.exp(last - logs)), spread[...])
        grad_scaled[rows, :] = tail * dot3(in_c, held[...])
        grad_in = dot3(tail * scaled[...], held[...], NT)
        reach = expand(of_heads(jnp.exp(logs)), spread[...])
        grad_out_map = dot3(reach * grad_ssd[rows, :], states[rows, :], NT)
        scores = dot3(in_c, out_c, NT)
        grad_scores = jnp.zeros((Q, Q), F32)
        for pair in range(8):
            lanes = slice(128 * pair, 128 * pair + 128)
            one, two = pair_gaps(logs, logs_t, pair, True)
            grad_pair = by_head(grad_ssd[rows, lanes], 0)
            weighted = jnp.concatenate([one * scores, two * scores], axis=1)
            grad_scaled[rows, lanes] = grad_scaled[rows, lanes] + dot3(weighted, grad_pair)
            both = dot3(scaled[:, lanes], grad_pair, NT)
            grad_scores = grad_scores + one * both[:, :Q] + two * both[:, Q:]
        grad_maps[rows, 0:128] = grad_in + dot3(grad_scores, out_c)
        grad_maps[rows, 128:256] = grad_out_map + dot3(grad_scores.T, in_c)
        held[...] = adjoint[rows, :] + through * held[...]
        return carry

    body(pl.program_id(0), 0)


def grad_kernel(
    tok_c, row, scale, gains, hp, spread, wide_c, gate_whole_c, grad_gate_c, value, in_map,
    step_raw, step, decay, fresh, through_all, states, grad_ssd, out_dot, grad_inner, grad_maps,
    crossings, adjoint_out, sums_mix,
    grad_wide, grad_steps, tokens_grad, sums, heads,
    after, grad_act_all, tok, wide, gate_whole, grad_gate,
):
    @pl.when(pl.program_id(0) == 0)
    def start():
        after[...] = jnp.ones_like(after)
        sums[...] = jnp.zeros_like(sums)
        heads[...] = jnp.zeros_like(heads)
        heads[2:3, :] = by_heads(sums_mix[...], spread[...])[1:2, :]

    skip = widen(hp[2:3, :], spread[...])
    chunks = scale.shape[0] // Q
    ones_up = (iota(1) >= iota(0)).astype(F32).astype(LOW)

    def body(i, carry):
        c = chunks - 1 - i
        rows = slice(None)
        place = rows_of(c)
        part = pl.ds(pl.multiple_of(c * 256, 256), 256)
        tok[place, :] = tok_c[...]
        grad_gate[place, :] = grad_gate_c[...]
        wide[part, :] = wide_c[...]
        gate_whole[part, :] = gate_whole_c[...]
        logs = decay[rows, :]
        last = logs[Q - 1 : Q, :]
        size = step[rows, :]
        through = through_all[eight(c), :][0:1, :]
        leaving = after[0:1, :] * adjoint_out[...]
        state_end = through * states[rows, :] + fresh[rows, :]
        crossing = jnp.sum(leaving * state_end, axis=0, keepdims=True)
        crossing = by_heads(jnp.broadcast_to(crossing, (8, 1024)), spread[...])
        crossing = (crossing + crossings[eight(c), :])[0:1, :]
        value_c = value[rows, :]
        sig = sigmoid(value_c)
        activated = value_c * sig
        size_wide = expand(size, spread[...])
        tail = expand(of_heads(jnp.exp(last - logs)), spread[...])
        grad_scaled = grad_inner[rows, :] + tail * dot3(in_map[rows, :], leaving)
        grad_in = grad_maps[rows, 0:128] + dot3(tail * (size_wide * activated), leaving, NT)
        per_step = by_heads(activated * grad_scaled, spread[...])
        grad_logs = out_dot[rows, :] - size * per_step
        grad_rate = select_left(ones_up, grad_logs) + crossing
        speed = jnp.exp(hp[1:2, :])
        raw = step_raw[rows, :]
        grad_raw = jnp.where(iota(1) < 16, (per_step - speed * grad_rate) * sigmoid(raw), 0.0)
        heads[0:1, :] = heads[0:1, :] + jnp.sum(grad_raw, axis=0, keepdims=True)
        heads[1:2, :] = heads[1:2, :] - jnp.sum(
            grad_rate * (speed * size), axis=0, keepdims=True
        )
        grad_act_c = size_wide * grad_scaled + skip * grad_ssd[rows, :]
        grad_wide[place, 0:1024] = (grad_act_c * sig * (1.0 + value_c * (1.0 - sig))).astype(LOW)
        grad_wide[place, 1024:1152] = grad_in.astype(LOW)
        grad_wide[place, 1152:1280] = grad_maps[rows, 128:256].astype(LOW)
        grad_steps[place, :] = grad_raw.astype(LOW)
        after[0:1, :] = after[0:1, :] * through
        return carry

    body(pl.program_id(0), 0)

    @pl.when(pl.program_id(0) == chunks - 1)
    def end():
        grad_act_all[...] = (
            dot(grad_wide[...], wide[:, :1280], NT)
            + dot(grad_steps[...], wide[:, 1280:1408], NT)
            + dot(grad_gate[...], gate_whole[...], NT)
        )

        def finish(c, carry):
            rows = rows_of(c)
            grad_act = grad_act_all[rows, :]
            factor = scale[rows, 0:1]
            normed = (tok[rows, :].astype(F32) + row[0:1, :]) * factor
            sums[0:1, :] = sums[0:1, :] + jnp.sum(grad_act * normed, axis=0, keepdims=True)
            grad_normed = grad_act * gains[0:1, :]
            mean = jnp.mean(grad_normed * normed, axis=1, keepdims=True)
            grad_input = factor * (grad_normed - normed * mean)
            tokens_grad[rows, :] = grad_input.astype(LOW)
            sums[1:2, :] = sums[1:2, :] + jnp.sum(grad_input, axis=0, keepdims=True)
            return carry

        lax.fori_loop(0, chunks, finish, 0)


def early_kernel(mine, other, packed):
    def body(j, carry):
        rows = pl.ds(pl.multiple_of(j * Q, Q), Q)
        both = mine[rows, :].astype(F32) + other[rows, :].astype(F32)
        packed[pl.ds(j * 16, 16)] = both.reshape(16, 8, -1).astype(LOW)
        return carry

    lax.fori_loop(0, mine.shape[0] // Q, body, 0)


def late_kernel(core_ref, term, steps, other, sums, sums_mix, tile, packed, across, columns):
    across[...] = jnp.zeros_like(across)
    across[16:17, :] = sums[0:1, :]
    across[17:18, :] = sums_mix[0:1, :]
    across[24:25, :] = sums[1:2, :]
    columns[...] = across[...].T
    first = core_ref[0] == 0
    lane = iota(1)

    def body(j, carry):
        rows = pl.ds(pl.multiple_of(j * Q, Q), Q)
        low, high = term[rows, 0:640].astype(F32), term[rows, 640:1280].astype(F32)
        mine = jnp.where(first, low, high)
        both = mine.astype(F32) + other[rows, :].astype(F32)
        packed[pl.ds(j * 16, 16), :, 0:640] = both.reshape(16, 8, 640).astype(LOW)
        extra = (steps[rows, :] + columns[rows, :]).reshape(16, 8, 128)
        extra = (extra + tile[...][None]).reshape(Q, 128)
        coarse = extra.astype(LOW).astype(F32)
        fine = pltpu.roll(extra - coarse, 64, 1)
        small = jnp.where(lane < 64, coarse, fine)
        packed[pl.ds(j * 16, 16), :, 640:768] = small.reshape(16, 8, 128).astype(LOW)
        return carry

    lax.fori_loop(0, term.shape[0] // Q, body, 0)


def early_sum(early, gates, outs):
    gates[...] = jnp.zeros_like(gates)
    outs[...] = jnp.zeros_like(outs)

    def body(j, carry):
        gates[...] += early[2 * j].astype(F32)
        outs[...] += early[2 * j + 1].astype(F32)
        return carry

    lax.fori_loop(0, early.shape[0] // 2, body, 0, unroll=4)


def late_sum(grad_scale, late, gates, outs, input_grad, output_grad, small, table):
    input_grad[...] = jnp.zeros_like(input_grad)
    small[...] = jnp.zeros_like(small)
    table[...] = jnp.zeros_like(table)
    input_grad[:, 0:1024] = gates[...] * grad_scale
    output_grad[...] = outs[...] * grad_scale
    lane = iota(1, (8, 128)).astype(F32)

    def body(j, carry):
        input_grad[:, 1024:1664] += late[2 * j, :, 0:640].astype(F32)
        input_grad[:, 1664:2304] += late[2 * j + 1, :, 0:640].astype(F32)
        for k in range(2):
            parts = late[2 * j + k, :, 640:768].astype(F32)
            parts = parts + pltpu.roll(parts, 64, 1)
            small[...] += parts
            table[...] += jnp.where(lane == parts[:, 25:26], parts[:, 24:25], 0.0)
        return carry

    lax.fori_loop(0, late.shape[0] // 2, body, 0, unroll=4)
    input_grad[:, 1024:2304] = input_grad[:, 1024:2304] * grad_scale
    small[...] = small[...] * grad_scale
    table[...] = table[...] * grad_scale


def at_origin(rank, *unused):
    return (0,) * rank


def run(kernel, args, outs, scratch=(), scalars=0, chunks=1, parts=(), out_parts=(), back=False):
    def spec(shape, divided):
        if not divided:
            return pl.BlockSpec(
                shape, functools.partial(at_origin, len(shape)), pipeline_mode=pl.Buffered(1)
            )
        block = (shape[0] // chunks,) + tuple(shape[1:])
        if back:
            return pl.BlockSpec(block, lambda i: (chunks - 1 - i, 0))
        return pl.BlockSpec(block, lambda i: (i, 0))

    return pl.pallas_call(
        kernel,
        name=getattr(kernel, "__name__", "late_sum"),
        out_shape=[jax.ShapeDtypeStruct(shape, dtype) for shape, dtype in outs],
        grid_spec=pltpu.PrefetchScalarGridSpec(
            num_scalar_prefetch=scalars,
            grid=(chunks,),
            in_specs=[spec(arg.shape, i in parts) for i, arg in enumerate(args[scalars:])],
            out_specs=[spec(shape, i in out_parts) for i, (shape, _) in enumerate(outs)],
            scratch_shapes=[pltpu.VMEM(shape, dtype) for shape, dtype in scratch],
        ),
        compiler_params=pltpu.CompilerParams(vmem_limit_bytes=60 << 20),
    )(*args)


def core_partner(value):
    flips = [(i, i ^ 1) for i in range(lax.axis_size("dp") * lax.axis_size("ctx"))]
    return lax.ppermute(value, ALL, flips)


def on_first_core():
    return lax.axis_index("ctx") % 2 == 0


def gather_rows(shard):
    half = shard.shape[0] // 2
    count = lax.axis_size("dp")
    mine = jnp.where(on_first_core(), shard[:half], shard[half:])
    pieces = lax.all_to_all(jnp.broadcast_to(mine[None], (count,) + mine.shape), "dp", 0, 0)
    return pieces, core_partner(pieces)


def moved(value, to):
    count = lax.axis_size("dp") * lax.axis_size("ctx")
    return lax.ppermute(value, ALL, [(i, to(i) % count) for i in range(count)])


def ring_near(mine):
    slots = lax.axis_size("ctx")
    return moved(mine, lambda i: i ^ slots)


def ring_sides(mine, near):
    step = 2 * lax.axis_size("ctx")
    even = lax.axis_index("dp") % 2 == 0
    pair = jnp.stack([jnp.where(even, mine, near), jnp.where(even, near, mine)])
    return pair, moved(pair, lambda i: i + step), moved(pair, lambda i: i - step)


def ring_far(lower, upper):
    step = 2 * lax.axis_size("ctx")
    half = lower.shape[1] // 2
    far_low = moved(lower[:, :half], lambda i: i + step)
    far_high = moved(upper[:, half:], lambda i: i - step)
    return far_low, far_high


def column_dot(a, b):
    return lax.dot_general(a, b, (((0,), (0,)), ((), ())), preferred_element_type=F32)


def per_device(
    tokens,
    grad_output,
    session_ids,
    session_table,
    norm_gain,
    input_weight,
    step_weight,
    head_params,
    gate_gain,
    output_weight,
):
    tok, grad_out = tokens[0], grad_output[0]
    bins = tok.shape[0]
    devices = lax.axis_size("dp") * lax.axis_size("ctx")
    slots = lax.axis_size("ctx")
    sessions = session_table.shape[0]
    grad_scale = 1.0 / math.sqrt(bins * devices)
    core = (lax.axis_index("ctx") % 2).astype(jnp.int32)[None]
    first = on_first_core()
    row = lax.dynamic_slice(session_table, (session_ids[0], 0), (1, 1024)).astype(F32)
    row = jnp.broadcast_to(row, (8, 1024))
    params = jnp.pad(head_params, ((0, 5), (0, 112)))
    copies = jnp.arange(128)[:, None]
    spread = ((jnp.arange(1024)[None, :] // 64 == copies % 16) & (copies < 48)).astype(LOW)
    shard = jnp.concatenate(
        [
            input_weight[:, 1024:],
            step_weight,
            norm_gain[:, None],
            gate_gain[:, None],
            jnp.zeros((input_weight.shape[0], 110), LOW),
        ],
        axis=1,
    )
    mine, other = gather_rows(shard)
    rest = jnp.concatenate([input_weight[:, :1024], output_weight], axis=1)
    rest_half = jnp.where(first, rest[:64], rest[64:])
    mine, rest_half = lax.optimization_barrier((mine, rest_half))
    near = ring_near(rest_half)
    place = jnp.stack([core[0], lax.axis_index("dp").astype(jnp.int32) // 2])
    seq = (bins, 1024)
    lane = (bins, 128)
    prepared = run(
        prep_kernel,
        (core, tok, row, mine, other, params, spread),
        (
            ((1024, 1408), LOW), (seq, LOW), (lane, F32), (seq, F32), (lane, F32), (lane, F32),
            (lane, F32), (lane, F32), (lane, F32), (seq, F32), ((128, 1152), F32), ((8, 1024), F32),
            ((bins // Q * 8, 1024), F32),
        ),
        (((128, 1024), F32), ((8, 128), F32), ((bins, 384), F32)),
        1,
    )
    wide, act_low, scale, value, in_map, out_map, step_raw, step = prepared[:8]
    decay, fresh, packed, gains, through = prepared[8:]
    near, packed = lax.optimization_barrier((near, packed))
    pair, lower, upper = ring_sides(rest_half, near)
    pieces = lax.all_to_all(packed.reshape(slots, 8, 1152), "ctx", 0, 0)
    y_local, states_local = run(
        local_kernel,
        (value, in_map, out_map, step, decay, fresh, through, spread),
        ((seq, F32), (seq, F32)),
        (((Q, 1024), F32), ((Q, 1024), F32), ((128, 1024), F32)),
        chunks=bins // Q,
        parts=range(6),
        out_parts=range(2),
    )
    pieces, y_local, lower, upper = lax.optimization_barrier((pieces, y_local, lower, upper))
    far_low, far_high = ring_far(lower, upper)
    carried, decays = run(
        scan_forward, (pieces, spread), (((slots, 8, 1024), F32), ((slots, 1024), F32))
    )
    carried, far_low, far_high = lax.optimization_barrier((carried, far_low, far_high))
    far = jnp.concatenate([far_low, far_high], axis=1)
    rest_mine = jnp.concatenate([pair, upper, far, lower], axis=0)
    rest_other = core_partner(rest_mine)
    state_in = lax.all_to_all(carried, "ctx", 0, 0).reshape(128, 1024)
    gate_whole, gate, grad_mixed = run(
        gate_kernel,
        (place, act_low, rest_mine, rest_other, grad_out),
        (((1024, 1024), LOW), (seq, F32), (seq, F32)),
        (((1024, 1024), LOW),),
        1,
    )
    mixed, grad_gate, grad_ssd, out_dot, adjoint, adjoint_local, states, sums_mix = run(
        mix_kernel,
        (
            gate, grad_mixed, value, out_map, decay, y_local, states_local, state_in, gains,
            params, through, spread,
        ),
        (
            (seq, LOW), (seq, LOW), (seq, F32), (lane, F32), (seq, F32), ((128, 1024), F32),
            (seq, F32), ((8, 1024), F32),
        ),
        (((8, 1024), F32),),
        chunks=bins // Q,
        parts=range(7),
        out_parts=(0, 1, 2, 3, 4, 6),
    )
    pieces = lax.all_to_all(adjoint_local.reshape(slots, 8, 1024), "ctx", 0, 0)
    grad_inner, grad_maps, crossings = run(
        inner_kernel,
        (
            spread, value, in_map, out_map, step, decay, fresh, through, states, grad_ssd,
            adjoint,
        ),
        ((seq, F32), ((bins, 256), F32), ((bins // Q * 8, 128), F32)),
        (((128, 1024), F32), ((Q, 1024), F32)),
        chunks=bins // Q,
        parts=(1, 2, 3, 4, 5, 6, 8, 9, 10),
        out_parts=range(2),
        back=True,
    )
    pieces, grad_inner = lax.optimization_barrier((pieces, grad_inner))
    (carried,) = run(scan_backward, (pieces, decays), (((slots, 8, 1024), F32),))
    carried, mixed, early_gate = lax.optimization_barrier((carried, mixed, grad_gate))
    term_output = column_dot(mixed, grad_out).astype(LOW)
    term_gates = column_dot(act_low, early_gate).astype(LOW)
    received = core_partner(jnp.where(first, term_output, term_gates))
    (early,) = run(
        early_kernel,
        (jnp.where(first, term_gates, term_output), received),
        (((devices, 8, 1024), LOW),),
    )
    adjoint_out = lax.all_to_all(carried, "ctx", 0, 0).reshape(128, 1024)
    adjoint_out, early = lax.optimization_barrier((adjoint_out, early))
    early_got = lax.all_to_all(early, ALL, 0, 0)
    grad_wide, grad_steps, tokens_grad, sums, heads = run(
        grad_kernel,
        (
            tok, row, scale, gains, params, spread, wide, gate_whole, grad_gate, value, in_map,
            step_raw, step, decay, fresh, through, states, grad_ssd, out_dot, grad_inner,
            grad_maps, crossings, adjoint_out, sums_mix,
        ),
        (
            ((bins, 1280), LOW), (lane, LOW), (seq, LOW), ((8, 1024), F32), ((8, 128), F32),
        ),
        (
            ((8, 1024), F32), (seq, F32), (seq, LOW), ((1024, 1408), LOW), ((1024, 1024), LOW),
            (seq, LOW),
        ),
        chunks=bins // Q,
        parts=(0, 6, 7, 8, 9, 10, 11, 12, 13, 14, 16, 17, 18, 19, 20),
        back=True,
    )
    term_low = column_dot(act_low, grad_wide).astype(LOW)
    term_steps = column_dot(act_low, grad_steps)
    received = core_partner(jnp.where(first, term_low[:, 640:], term_low[:, :640]))
    tile = jnp.concatenate(
        [
            jnp.zeros((8, 18), F32),
            heads[:3, :16].reshape(8, 6),
            jnp.zeros((8, 1), F32),
            jnp.broadcast_to(session_ids.astype(F32)[:, None], (8, 1)),
            jnp.zeros((8, 102), F32),
        ],
        axis=1,
    )
    (late,) = run(
        late_kernel,
        (core, term_low, term_steps, received, sums, sums_mix, tile),
        (((devices, 8, 768), LOW),),
        (((128, 1024), F32), ((1024, 128), F32)),
        1,
    )
    late_got = lax.all_to_all(late, ALL, 0, 0)
    gates, outs = run(early_sum, (early_got,), (((8, 1024), F32), ((8, 1024), F32)))
    input_grad, output_grad, totals, table = run(
        functools.partial(late_sum, grad_scale),
        (late_got, gates, outs),
        (((8, 2304), F32), ((8, 1024), F32), ((8, 128), F32), ((8, 128), F32)),
    )
    return (
        tokens_grad[None],
        totals[:, 16],
        input_grad,
        totals[:, :16],
        totals[:, 18:24].reshape(3, 16),
        totals[:, 17],
        output_grad,
        table[:, :sessions].T,
    )


def solution(mesh):
    placed = (
        P("dp", "ctx", None),
        P("dp", "ctx", None),
        P("dp"),
        P(),
        P("dp"),
        P("dp", None),
        P("dp", None),
        P(),
        P("dp"),
        P("dp", None),
    )
    return jax.shard_map(
        per_device,
        mesh=mesh,
        in_specs=placed,
        out_specs=(
            P("dp", "ctx", None),
            P(("dp", "ctx")),
            P(("dp", "ctx"), None),
            P(("dp", "ctx"), None),
            P(),
            P(("dp", "ctx")),
            P(("dp", "ctx"), None),
            P(None, ("dp", "ctx")),
        ),
        check_vma=False,
    )
```

```python
import functools
import math

import jax
import jax.numpy as jnp
from jax import lax
from jax.experimental import pallas as pl
from jax.experimental.pallas import tpu as pltpu
from jax.sharding import PartitionSpec as P

epsilon = 1e-05
ALL = ("dp", "ctx")
Q = 128
F32 = jnp.float32
LOW = jnp.bfloat16
NN = (((1,), (0,)), ((), ()))
NT = (((1,), (1,)), ((), ()))


def dot(a, b, dims=NN):
    return lax.dot_general(a, b, dims, preferred_element_type=F32)


def split(x):
    high = x.astype(LOW)
    return high, (x - high.astype(F32)).astype(LOW)


def dot3(a, b, dims=NN):
    (ah, al), (bh, bl) = split(a), split(b)
    return dot(ah, bh, dims) + dot(ah, bl, dims) + dot(al, bh, dims)


def thirds(x):
    high = x.astype(LOW)
    rest = x - high.astype(F32)
    mid = rest.astype(LOW)
    return high, mid, (rest - mid.astype(F32)).astype(LOW)


def expand(x, spread):
    high = x.astype(LOW).astype(F32)
    rest = x - high
    mid = rest.astype(LOW).astype(F32)
    parts = high + pltpu.roll(mid, 16, 1) + pltpu.roll(rest - mid, 32, 1)
    return dot(parts.astype(LOW), spread)


def by_heads(x, spread):
    high, low = split(x)
    return dot(high, spread, NT) + dot(low, spread, NT)


def of_heads(x):
    return jnp.where(iota(1, x.shape) < 16, x, 0.0)


def select_left(chosen, x):
    high, mid, low = thirds(x)
    return dot(chosen, high) + dot(chosen, mid) + dot(chosen, low)


def sigmoid(x):
    return 1.0 / (1.0 + jnp.exp(-x))


def softplus(x):
    u = jnp.exp(-jnp.abs(x))
    w = 1.0 + u
    log1p = jnp.where(w == 1.0, u, jnp.log(w) * (u / jnp.where(w == 1.0, 1.0, w - 1.0)))
    return jnp.maximum(x, 0.0) + log1p


def iota(dim, shape=(Q, Q)):
    return lax.broadcasted_iota(jnp.int32, shape, dim)


def rows_of(c):
    return pl.ds(pl.multiple_of(c * Q, Q), Q)


def assemble(core, mine, other, whole):
    half = mine.shape[1]
    first = pl.multiple_of(core * half, half)
    second = pl.multiple_of((1 - core) * half, half)
    for i in range(mine.shape[0]):
        whole[pl.ds(2 * half * i + first, half), :] = mine[i]
        whole[pl.ds(2 * half * i + second, half), :] = other[i]


def prep_kernel(
    core_ref, tok, row, mine, other, hp, spread,
    wide, act_low, scale, value, in_map, out_map, step_raw, step, decay, fresh, packed, gains,
    through,
    state, total, rest,
):
    assemble(core_ref[0], mine, other, wide)
    small = wide[:, 1280:1408].astype(F32).T
    gains[0:1, :] = small[16:17, :]
    gains[1:2, :] = small[17:18, :]
    state[...] = jnp.zeros_like(state)
    total[...] = jnp.zeros_like(total)
    ones_low = (iota(0) >= iota(1)).astype(F32).astype(LOW)
    chunks = tok.shape[0] // Q

    def norm(c, carry):
        rows = rows_of(c)
        x = tok[rows, :].astype(F32) + row[0:1, :]
        factor = lax.rsqrt(jnp.mean(x * x, axis=1, keepdims=True) + epsilon)
        act_low[rows, :] = (x * factor * gains[0:1, :]).astype(LOW)
        scale[rows, :] = jnp.broadcast_to(factor, (Q, 128))
        return carry

    lax.fori_loop(0, chunks, norm, 0)
    value[...] = dot(act_low[...], wide[:, :1024])
    rest[...] = dot(act_low[...], wide[:, 1024:1408])

    def body(c, carry):
        rows = rows_of(c)
        value_c = value[rows, :]
        in_c = rest[rows, 0:128]
        in_map[rows, :] = in_c
        out_map[rows, :] = rest[rows, 128:256]
        raw = of_heads(rest[rows, 256:384] + hp[0:1, :])
        step_raw[rows, :] = raw
        size = of_heads(softplus(raw))
        step[rows, :] = size
        logs = select_left(ones_low, -jnp.exp(hp[1:2, :]) * size)
        decay[rows, :] = logs
        last = logs[Q - 1 : Q, :]
        weight = expand(jnp.exp(last - logs) * size, spread[...])
        activated = value_c * sigmoid(value_c)
        fresh_c = dot3(in_c.T, weight * activated)
        fresh[rows, :] = fresh_c
        kept = expand(of_heads(jnp.broadcast_to(jnp.exp(last), (8, 128))), spread[...])
        through[eight(c), :] = kept
        state[...] = kept[0:1, :] * state[...] + fresh_c
        total[...] = total[...] + last
        return carry

    lax.fori_loop(0, chunks, body, 0)
    packed[:, :1024] = state[...]
    packed[:, 1024:1152] = jnp.broadcast_to(jnp.exp(total[0:1, :]), (128, 128))


def scan_forward(pieces, spread, carried, decays):
    count = pieces.shape[0]
    rates = jnp.concatenate([pieces[j, 0:1, 1024:1152] for j in range(count)], axis=0)
    decays[...] = expand(of_heads(rates), spread[...])
    held = jnp.zeros((8, 1024), F32)
    for j in range(count):
        carried[j] = held
        held = decays[j : j + 1, :] * held + pieces[j, :, :1024]


def scan_backward(pieces, decays, carried):
    count = pieces.shape[0]
    held = jnp.zeros((8, 1024), F32)
    for j in range(count - 1, -1, -1):
        carried[j] = held
        held = decays[j : j + 1, :] * held + pieces[j]


def pair_gaps(logs, logs_t, pair, transposed):
    gaps = []
    for head in (2 * pair, 2 * pair + 1):
        column = jnp.broadcast_to(logs[:, head : head + 1], (Q, Q))
        across = jnp.broadcast_to(logs_t[head : head + 1, :], (Q, Q))
        if transposed:
            gap = jnp.where(iota(1) >= iota(0), across - column, -1e30)
        else:
            gap = jnp.where(iota(0) >= iota(1), column - across, -1e30)
        gaps.append(jnp.exp(gap))
    return gaps


def by_head(x, axis):
    first = iota(1) < 64
    return jnp.concatenate([jnp.where(first, x, 0.0), jnp.where(first, 0.0, x)], axis=axis)


def widen(row, spread):
    return expand(jnp.broadcast_to(row, (8, 128)), spread)[0:1, :]


def eight(c):
    return pl.ds(pl.multiple_of(8 * c, 8), 8)


def local_kernel(value, in_map, out_map, step, decay, fresh, through, spread, y_local, states, ssd, scaled, held):
    @pl.when(pl.program_id(0) == 0)
    def start():
        held[...] = jnp.zeros_like(held)

    def body(c, carry):
        rows = slice(None)
        states[rows, :] = held[...]
        logs = decay[rows, :]
        logs_t = logs.T
        value_c = value[rows, :]
        scaled[...] = expand(step[rows, :], spread[...]) * (value_c * sigmoid(value_c))
        reach = expand(of_heads(jnp.exp(logs)), spread[...])
        out_c = out_map[rows, :]
        scores = dot3(out_c, in_map[rows, :], NT)
        for pair in range(8):
            lanes = slice(128 * pair, 128 * pair + 128)
            one, two = pair_gaps(logs, logs_t, pair, False)
            weighted = jnp.concatenate([one * scores, two * scores], axis=1)
            ssd[:, lanes] = dot3(weighted, by_head(scaled[:, lanes], 0))
        y_local[rows, :] = ssd[...] + reach * dot3(out_c, held[...])
        held[...] = through[eight(c), :][0:1, :] * held[...] + fresh[rows, :]
        return carry

    body(pl.program_id(0), 0)


def gate_kernel(
    place_ref, act_low, mine, other, grad_out, gate_whole, gate, grad_mixed, out_whole
):
    core, group = place_ref[0], place_ref[1]
    half = mine.shape[1]
    for i in range(mine.shape[0]):
        start = ((group + i // 2) % 4 * 2 + i % 2) * (2 * half)
        for block, turn in ((mine, core), (other, 1 - core)):
            rows = pl.ds(pl.multiple_of(start + turn * half, half), half)
            gate_whole[rows, :] = block[i, :, :1024]
            out_whole[rows, :] = block[i, :, 1024:]
    gate[...] = dot(act_low[...], gate_whole[...])
    grad_mixed[...] = dot(grad_out[...], out_whole[...], NT)


def mix_kernel(
    gate_all, grad_mixed_all, value, out_map, decay, y_local, states_local, state_in, gains, hp,
    through, spread,
    mixed, grad_gate, grad_ssd, out_dot, adjoint, adjoint_local, states, sums,
    base,
):
    @pl.when(pl.program_id(0) == 0)
    def start():
        base[...] = jnp.ones_like(base)
        adjoint_local[...] = jnp.zeros_like(adjoint_local)
        sums[...] = jnp.zeros_like(sums)

    skip = widen(hp[2:3, :], spread[...])

    def body(c, carry):
        rows = slice(None)
        before = base[0:1, :]
        entering = before * state_in[...]
        states[rows, :] = states_local[rows, :] + entering
        logs = decay[rows, :]
        value_c = value[rows, :]
        activated = value_c * sigmoid(value_c)
        reach = expand(of_heads(jnp.exp(logs)), spread[...])
        out_c = out_map[rows, :]
        y_state = y_local[rows, :] + reach * dot3(out_c, entering)
        y = y_state + skip * activated
        gate = gate_all[rows, :]
        grad_mixed = grad_mixed_all[rows, :]
        sig = sigmoid(gate)
        silu = gate * sig
        gated = y * silu
        gate_scale = lax.rsqrt(jnp.mean(gated * gated, axis=1, keepdims=True) + epsilon)
        gnorm = gated * gate_scale
        mixed[rows, :] = (gnorm * gains[1:2, :]).astype(LOW)
        along = grad_mixed * gnorm
        sums[0:1, :] = sums[0:1, :] + jnp.sum(along, axis=0, keepdims=True)
        grad_gnorm = grad_mixed * gains[1:2, :]
        mean = jnp.mean(grad_gnorm * gnorm, axis=1, keepdims=True)
        grad_gated = gate_scale * (grad_gnorm - gnorm * mean)
        grad_gate[rows, :] = (grad_gated * y * sig * (1.0 + gate * (1.0 - sig))).astype(LOW)
        grad_y = grad_gated * silu
        grad_ssd[rows, :] = grad_y
        sums[1:2, :] = sums[1:2, :] + jnp.sum(grad_y * activated, axis=0, keepdims=True)
        out_dot[rows, :] = by_heads(grad_y * y_state, spread[...])
        adjoint_c = dot3(out_c.T, reach * grad_y)
        adjoint[rows, :] = adjoint_c
        adjoint_local[...] = adjoint_local[...] + before * adjoint_c
        base[0:1, :] = before * through[eight(c), :][0:1, :]
        return carry

    body(pl.program_id(0), 0)


def inner_kernel(
    spread, value, in_map, out_map, step, decay, fresh, through_all, states, grad_ssd, adjoint,
    grad_scaled, grad_maps, crossings,
    held, scaled,
):
    chunks = pl.num_programs(0)

    @pl.when(pl.program_id(0) == 0)
    def start():
        held[...] = jnp.zeros_like(held)

    def body(i, carry):
        c = chunks - 1 - i
        rows = slice(None)
        logs = decay[rows, :]
        logs_t = logs.T
        last = logs[Q - 1 : Q, :]
        in_c = in_map[rows, :]
        out_c = out_map[rows, :]
        through = through_all[eight(c), :][0:1, :]
        state_end = through * states[rows, :] + fresh[rows, :]
        crossing = jnp.sum(held[...] * state_end, axis=0, keepdims=True)
        crossing = by_heads(jnp.broadcast_to(crossing, (8, 1024)), spread[...])
        crossings[eight(c), :] = crossing
        value_c = value[rows, :]
        scaled[...] = expand(step[rows, :], spread[...]) * (value_c * sigmoid(value_c))
        tail = expand(of_heads(jnp.exp(last - logs)), spread[...])
        grad_scaled[rows, :] = tail * dot3(in_c, held[...])
        grad_in = dot3(tail * scaled[...], held[...], NT)
        reach = expand(of_heads(jnp.exp(logs)), spread[...])
        grad_out_map = dot3(reach * grad_ssd[rows, :], states[rows, :], NT)
        scores = dot3(in_c, out_c, NT)
        grad_scores = jnp.zeros((Q, Q), F32)
        for pair in range(8):
            lanes = slice(128 * pair, 128 * pair + 128)
            one, two = pair_gaps(logs, logs_t, pair, True)
            grad_pair = by_head(grad_ssd[rows, lanes], 0)
            weighted = jnp.concatenate([one * scores, two * scores], axis=1)
            grad_scaled[rows, lanes] = grad_scaled[rows, lanes] + dot3(weighted, grad_pair)
            both = dot3(scaled[:, lanes], grad_pair, NT)
            grad_scores = grad_scores + one * both[:, :Q] + two * both[:, Q:]
        grad_maps[rows, 0:128] = grad_in + dot3(grad_scores, out_c)
        grad_maps[rows, 128:256] = grad_out_map + dot3(grad_scores.T, in_c)
        held[...] = adjoint[rows, :] + through * held[...]
        return carry

    body(pl.program_id(0), 0)


def grad_kernel(
    tok_c, row, scale, gains, hp, spread, wide_c, gate_whole_c, grad_gate_c, value, in_map,
    step_raw, step, decay, fresh, through_all, states, grad_ssd, out_dot, grad_inner, grad_maps,
    crossings, adjoint_out, sums_mix,
    grad_wide, grad_steps, tokens_grad, sums, heads,
    after, grad_act_all, tok, wide, gate_whole, grad_gate,
):
    @pl.when(pl.program_id(0) == 0)
    def start():
        after[...] = jnp.ones_like(after)
        sums[...] = jnp.zeros_like(sums)
        heads[...] = jnp.zeros_like(heads)
        heads[2:3, :] = by_heads(sums_mix[...], spread[...])[1:2, :]

    skip = widen(hp[2:3, :], spread[...])
    chunks = scale.shape[0] // Q
    ones_up = (iota(1) >= iota(0)).astype(F32).astype(LOW)

    def body(i, carry):
        c = chunks - 1 - i
        rows = slice(None)
        place = rows_of(c)
        part = pl.ds(pl.multiple_of(c * 256, 256), 256)
        tok[place, :] = tok_c[...]
        grad_gate[place, :] = grad_gate_c[...]
        wide[part, :] = wide_c[...]
        gate_whole[part, :] = gate_whole_c[...]
        logs = decay[rows, :]
        last = logs[Q - 1 : Q, :]
        size = step[rows, :]
        through = through_all[eight(c), :][0:1, :]
        leaving = after[0:1, :] * adjoint_out[...]
        state_end = through * states[rows, :] + fresh[rows, :]
        crossing = jnp.sum(leaving * state_end, axis=0, keepdims=True)
        crossing = by_heads(jnp.broadcast_to(crossing, (8, 1024)), spread[...])
        crossing = (crossing + crossings[eight(c), :])[0:1, :]
        value_c = value[rows, :]
        sig = sigmoid(value_c)
        activated = value_c * sig
        size_wide = expand(size, spread[...])
        tail = expand(of_heads(jnp.exp(last - logs)), spread[...])
        grad_scaled = grad_inner[rows, :] + tail * dot3(in_map[rows, :], leaving)
        grad_in = grad_maps[rows, 0:128] + dot3(tail * (size_wide * activated), leaving, NT)
        per_step = by_heads(activated * grad_scaled, spread[...])
        grad_logs = out_dot[rows, :] - size * per_step
        grad_rate = select_left(ones_up, grad_logs) + crossing
        speed = jnp.exp(hp[1:2, :])
        raw = step_raw[rows, :]
        grad_raw = jnp.where(iota(1) < 16, (per_step - speed * grad_rate) * sigmoid(raw), 0.0)
        heads[0:1, :] = heads[0:1, :] + jnp.sum(grad_raw, axis=0, keepdims=True)
        heads[1:2, :] = heads[1:2, :] - jnp.sum(
            grad_rate * (speed * size), axis=0, keepdims=True
        )
        grad_act_c = size_wide * grad_scaled + skip * grad_ssd[rows, :]
        grad_wide[place, 0:1024] = (grad_act_c * sig * (1.0 + value_c * (1.0 - sig))).astype(LOW)
        grad_wide[place, 1024:1152] = grad_in.astype(LOW)
        grad_wide[place, 1152:1280] = grad_maps[rows, 128:256].astype(LOW)
        grad_steps[place, :] = grad_raw.astype(LOW)
        after[0:1, :] = after[0:1, :] * through
        return carry

    body(pl.program_id(0), 0)

    @pl.when(pl.program_id(0) == chunks - 1)
    def end():
        grad_act_all[...] = (
            dot(grad_wide[...], wide[:, :1280], NT)
            + dot(grad_steps[...], wide[:, 1280:1408], NT)
            + dot(grad_gate[...], gate_whole[...], NT)
        )

        def finish(c, carry):
            rows = rows_of(c)
            grad_act = grad_act_all[rows, :]
            factor = scale[rows, 0:1]
            normed = (tok[rows, :].astype(F32) + row[0:1, :]) * factor
            sums[0:1, :] = sums[0:1, :] + jnp.sum(grad_act * normed, axis=0, keepdims=True)
            grad_normed = grad_act * gains[0:1, :]
            mean = jnp.mean(grad_normed * normed, axis=1, keepdims=True)
            grad_input = factor * (grad_normed - normed * mean)
            tokens_grad[rows, :] = grad_input.astype(LOW)
            sums[1:2, :] = sums[1:2, :] + jnp.sum(grad_input, axis=0, keepdims=True)
            return carry

        lax.fori_loop(0, chunks, finish, 0)


def early_kernel(mine, other, packed):
    def body(j, carry):
        rows = pl.ds(pl.multiple_of(j * Q, Q), Q)
        both = mine[rows, :].astype(F32) + other[rows, :].astype(F32)
        packed[pl.ds(j * 16, 16)] = both.reshape(16, 8, -1).astype(LOW)
        return carry

    lax.fori_loop(0, mine.shape[0] // Q, body, 0)


def late_kernel(core_ref, term, steps, other, sums, sums_mix, tile, packed, across, columns):
    @pl.when(pl.program_id(0) == 0)
    def start():
        across[...] = jnp.zeros_like(across)
        across[16:17, :] = sums[0:1, :]
        across[17:18, :] = sums_mix[0:1, :]
        across[24:25, :] = sums[1:2, :]
        columns[...] = across[...].T

    first = core_ref[0] == 0
    low, high = term[:, 0:640].astype(F32), term[:, 640:1280].astype(F32)
    both = jnp.where(first, low, high) + other[...].astype(F32)
    packed[:, :, 0:640] = both.reshape(16, 8, 640).astype(LOW)
    extra = (steps[...] + columns[rows_of(pl.program_id(0)), :]).reshape(16, 8, 128)
    extra = (extra + tile[...][None]).reshape(Q, 128)
    coarse = extra.astype(LOW).astype(F32)
    fine = pltpu.roll(extra - coarse, 64, 1)
    small = jnp.where(iota(1) < 64, coarse, fine)
    packed[:, :, 640:768] = small.reshape(16, 8, 128).astype(LOW)


def early_sum(early, gates, outs):
    gates[...] = jnp.zeros_like(gates)
    outs[...] = jnp.zeros_like(outs)

    def body(j, carry):
        gates[...] += early[2 * j].astype(F32)
        outs[...] += early[2 * j + 1].astype(F32)
        return carry

    lax.fori_loop(0, early.shape[0] // 2, body, 0, unroll=4)


def late_sum(grad_scale, late, gates, outs, input_grad, output_grad, small, table):
    input_grad[...] = jnp.zeros_like(input_grad)
    small[...] = jnp.zeros_like(small)
    table[...] = jnp.zeros_like(table)
    input_grad[:, 0:1024] = gates[...] * grad_scale
    output_grad[...] = outs[...] * grad_scale
    lane = iota(1, (8, 128)).astype(F32)
    across = late.shape[0] // 8

    def body(d, carry):
        parts = jnp.zeros((8, 128), F32)
        low = jnp.zeros((8, 640), F32)
        high = jnp.zeros((8, 640), F32)
        for k in range(0, across, 2):
            even, odd = late[across * d + k], late[across * d + k + 1]
            low = low + even[:, 0:640].astype(F32)
            high = high + odd[:, 0:640].astype(F32)
            parts = parts + even[:, 640:768].astype(F32) + odd[:, 640:768].astype(F32)
        input_grad[:, 1024:1664] += low
        input_grad[:, 1664:2304] += high
        parts = parts + pltpu.roll(parts, 64, 1)
        small[...] += parts
        session = parts[:, 25:26] * (1.0 / across)
        table[...] += jnp.where(lane == session, parts[:, 24:25], 0.0)
        return carry

    lax.fori_loop(0, 8, body, 0)
    input_grad[:, 1024:2304] = input_grad[:, 1024:2304] * grad_scale
    small[...] = small[...] * grad_scale
    table[...] = table[...] * grad_scale


def at_origin(rank, *unused):
    return (0,) * rank


def run(kernel, args, outs, scratch=(), scalars=0, chunks=1, parts=(), out_parts=(), back=False):
    def spec(shape, divided):
        if not divided:
            return pl.BlockSpec(
                shape, functools.partial(at_origin, len(shape)), pipeline_mode=pl.Buffered(1)
            )
        block = (shape[0] // chunks,) + tuple(shape[1:])
        last = (0,) * (len(shape) - 1)
        if back:
            return pl.BlockSpec(block, lambda i, *unused: (chunks - 1 - i,) + last)
        return pl.BlockSpec(block, lambda i, *unused: (i,) + last)

    return pl.pallas_call(
        kernel,
        name=getattr(kernel, "__name__", "late_sum"),
        out_shape=[jax.ShapeDtypeStruct(shape, dtype) for shape, dtype in outs],
        grid_spec=pltpu.PrefetchScalarGridSpec(
            num_scalar_prefetch=scalars,
            grid=(chunks,),
            in_specs=[spec(arg.shape, i in parts) for i, arg in enumerate(args[scalars:])],
            out_specs=[spec(shape, i in out_parts) for i, (shape, _) in enumerate(outs)],
            scratch_shapes=[pltpu.VMEM(shape, dtype) for shape, dtype in scratch],
        ),
        compiler_params=pltpu.CompilerParams(vmem_limit_bytes=60 << 20),
    )(*args)


def core_partner(value):
    flips = [(i, i ^ 1) for i in range(lax.axis_size("dp") * lax.axis_size("ctx"))]
    return lax.ppermute(value, ALL, flips)


def on_first_core():
    return lax.axis_index("ctx") % 2 == 0


def gather_rows(shard):
    half = shard.shape[0] // 2
    count = lax.axis_size("dp")
    mine = jnp.where(on_first_core(), shard[:half], shard[half:])
    pieces = lax.all_to_all(jnp.broadcast_to(mine[None], (count,) + mine.shape), "dp", 0, 0)
    return pieces, core_partner(pieces)


def moved(value, to):
    count = lax.axis_size("dp") * lax.axis_size("ctx")
    return lax.ppermute(value, ALL, [(i, to(i) % count) for i in range(count)])


def ring_near(mine):
    slots = lax.axis_size("ctx")
    return moved(mine, lambda i: i ^ slots)


def ring_sides(mine, near):
    step = 2 * lax.axis_size("ctx")
    even = lax.axis_index("dp") % 2 == 0
    pair = jnp.stack([jnp.where(even, mine, near), jnp.where(even, near, mine)])
    return pair, moved(pair, lambda i: i + step), moved(pair, lambda i: i - step)


def ring_far(lower, upper):
    step = 2 * lax.axis_size("ctx")
    half = lower.shape[1] // 2
    far_low = moved(lower[:, :half], lambda i: i + step)
    far_high = moved(upper[:, half:], lambda i: i - step)
    return far_low, far_high


def column_dot(a, b):
    return lax.dot_general(a, b, (((0,), (0,)), ((), ())), preferred_element_type=F32)


def per_device(
    tokens,
    grad_output,
    session_ids,
    session_table,
    norm_gain,
    input_weight,
    step_weight,
    head_params,
    gate_gain,
    output_weight,
):
    tok, grad_out = tokens[0], grad_output[0]
    bins = tok.shape[0]
    devices = lax.axis_size("dp") * lax.axis_size("ctx")
    slots = lax.axis_size("ctx")
    sessions = session_table.shape[0]
    grad_scale = 1.0 / math.sqrt(bins * devices)
    core = (lax.axis_index("ctx") % 2).astype(jnp.int32)[None]
    first = on_first_core()
    row = lax.dynamic_slice(session_table, (session_ids[0], 0), (1, 1024)).astype(F32)
    row = jnp.broadcast_to(row, (8, 1024))
    params = jnp.pad(head_params, ((0, 5), (0, 112)))
    copies = jnp.arange(128)[:, None]
    spread = ((jnp.arange(1024)[None, :] // 64 == copies % 16) & (copies < 48)).astype(LOW)
    shard = jnp.concatenate(
        [
            input_weight[:, 1024:],
            step_weight,
            norm_gain[:, None],
            gate_gain[:, None],
            jnp.zeros((input_weight.shape[0], 110), LOW),
        ],
        axis=1,
    )
    mine, other = gather_rows(shard)
    rest = jnp.concatenate([input_weight[:, :1024], output_weight], axis=1)
    rest_half = jnp.where(first, rest[:64], rest[64:])
    mine, rest_half = lax.optimization_barrier((mine, rest_half))
    near = ring_near(rest_half)
    place = jnp.stack([core[0], lax.axis_index("dp").astype(jnp.int32) // 2])
    seq = (bins, 1024)
    lane = (bins, 128)
    prepared = run(
        prep_kernel,
        (core, tok, row, mine, other, params, spread),
        (
            ((1024, 1408), LOW), (seq, LOW), (lane, F32), (seq, F32), (lane, F32), (lane, F32),
            (lane, F32), (lane, F32), (lane, F32), (seq, F32), ((128, 1152), F32), ((8, 1024), F32),
            ((bins // Q * 8, 1024), F32),
        ),
        (((128, 1024), F32), ((8, 128), F32), ((bins, 384), F32)),
        1,
    )
    wide, act_low, scale, value, in_map, out_map, step_raw, step = prepared[:8]
    decay, fresh, packed, gains, through = prepared[8:]
    near, packed = lax.optimization_barrier((near, packed))
    pair, lower, upper = ring_sides(rest_half, near)
    pieces = lax.all_to_all(packed.reshape(slots, 8, 1152), "ctx", 0, 0)
    y_local, states_local = run(
        local_kernel,
        (value, in_map, out_map, step, decay, fresh, through, spread),
        ((seq, F32), (seq, F32)),
        (((Q, 1024), F32), ((Q, 1024), F32), ((128, 1024), F32)),
        chunks=bins // Q,
        parts=range(6),
        out_parts=range(2),
    )
    pieces, y_local, lower, upper = lax.optimization_barrier((pieces, y_local, lower, upper))
    far_low, far_high = ring_far(lower, upper)
    carried, decays = run(
        scan_forward, (pieces, spread), (((slots, 8, 1024), F32), ((slots, 1024), F32))
    )
    carried, far_low, far_high = lax.optimization_barrier((carried, far_low, far_high))
    far = jnp.concatenate([far_low, far_high], axis=1)
    rest_mine = jnp.concatenate([pair, upper, far, lower], axis=0)
    rest_other = core_partner(rest_mine)
    state_in = lax.all_to_all(carried, "ctx", 0, 0).reshape(128, 1024)
    gate_whole, gate, grad_mixed = run(
        gate_kernel,
        (place, act_low, rest_mine, rest_other, grad_out),
        (((1024, 1024), LOW), (seq, F32), (seq, F32)),
        (((1024, 1024), LOW),),
        1,
    )
    mixed, grad_gate, grad_ssd, out_dot, adjoint, adjoint_local, states, sums_mix = run(
        mix_kernel,
        (
            gate, grad_mixed, value, out_map, decay, y_local, states_local, state_in, gains,
            params, through, spread,
        ),
        (
            (seq, LOW), (seq, LOW), (seq, F32), (lane, F32), (seq, F32), ((128, 1024), F32),
            (seq, F32), ((8, 1024), F32),
        ),
        (((8, 1024), F32),),
        chunks=bins // Q,
        parts=range(7),
        out_parts=(0, 1, 2, 3, 4, 6),
    )
    pieces = lax.all_to_all(adjoint_local.reshape(slots, 8, 1024), "ctx", 0, 0)
    grad_inner, grad_maps, crossings = run(
        inner_kernel,
        (
            spread, value, in_map, out_map, step, decay, fresh, through, states, grad_ssd,
            adjoint,
        ),
        ((seq, F32), ((bins, 256), F32), ((bins // Q * 8, 128), F32)),
        (((128, 1024), F32), ((Q, 1024), F32)),
        chunks=bins // Q,
        parts=(1, 2, 3, 4, 5, 6, 8, 9, 10),
        out_parts=range(2),
        back=True,
    )
    pieces, grad_inner = lax.optimization_barrier((pieces, grad_inner))
    (carried,) = run(scan_backward, (pieces, decays), (((slots, 8, 1024), F32),))
    carried, mixed, early_gate = lax.optimization_barrier((carried, mixed, grad_gate))
    term_output = column_dot(mixed, grad_out).astype(LOW)
    term_gates = column_dot(act_low, early_gate).astype(LOW)
    received = core_partner(jnp.where(first, term_output, term_gates))
    (early,) = run(
        early_kernel,
        (jnp.where(first, term_gates, term_output), received),
        (((devices, 8, 1024), LOW),),
    )
    adjoint_out = lax.all_to_all(carried, "ctx", 0, 0).reshape(128, 1024)
    adjoint_out, early = lax.optimization_barrier((adjoint_out, early))
    early_got = lax.all_to_all(early, ALL, 0, 0)
    grad_wide, grad_steps, tokens_grad, sums, heads = run(
        grad_kernel,
        (
            tok, row, scale, gains, params, spread, wide, gate_whole, grad_gate, value, in_map,
            step_raw, step, decay, fresh, through, states, grad_ssd, out_dot, grad_inner,
            grad_maps, crossings, adjoint_out, sums_mix,
        ),
        (
            ((bins, 1280), LOW), (lane, LOW), (seq, LOW), ((8, 1024), F32), ((8, 128), F32),
        ),
        (
            ((8, 1024), F32), (seq, F32), (seq, LOW), ((1024, 1408), LOW), ((1024, 1024), LOW),
            (seq, LOW),
        ),
        chunks=bins // Q,
        parts=(0, 6, 7, 8, 9, 10, 11, 12, 13, 14, 16, 17, 18, 19, 20),
        back=True,
    )
    term_low = column_dot(act_low, grad_wide).astype(LOW)
    term_steps = column_dot(act_low, grad_steps)
    received = core_partner(jnp.where(first, term_low[:, 640:], term_low[:, :640]))
    tile = jnp.concatenate(
        [
            jnp.zeros((8, 18), F32),
            heads[:3, :16].reshape(8, 6),
            jnp.zeros((8, 1), F32),
            jnp.broadcast_to(session_ids.astype(F32)[:, None], (8, 1)),
            jnp.zeros((8, 102), F32),
        ],
        axis=1,
    )
    (late,) = run(
        late_kernel,
        (core, term_low, term_steps, received, sums, sums_mix, tile),
        (((devices, 8, 768), LOW),),
        (((128, 1024), F32), ((1024, 128), F32)),
        1,
        chunks=1024 // Q,
        parts=range(3),
        out_parts=(0,),
    )
    late_got = lax.all_to_all(late, ALL, 0, 0)
    gates, outs = run(early_sum, (early_got,), (((8, 1024), F32), ((8, 1024), F32)))
    input_grad, output_grad, totals, table = run(
        functools.partial(late_sum, grad_scale),
        (late_got, gates, outs),
        (((8, 2304), F32), ((8, 1024), F32), ((8, 128), F32), ((8, 128), F32)),
    )
    return (
        tokens_grad[None],
        totals[:, 16],
        input_grad,
        totals[:, :16],
        totals[:, 18:24].reshape(3, 16),
        totals[:, 17],
        output_grad,
        table[:, :sessions].T,
    )


def solution(mesh):
    placed = (
        P("dp", "ctx", None),
        P("dp", "ctx", None),
        P("dp"),
        P(),
        P("dp"),
        P("dp", None),
        P("dp", None),
        P(),
        P("dp"),
        P("dp", None),
    )
    return jax.shard_map(
        per_device,
        mesh=mesh,
        in_specs=placed,
        out_specs=(
            P("dp", "ctx", None),
            P(("dp", "ctx")),
            P(("dp", "ctx"), None),
            P(("dp", "ctx"), None),
            P(),
            P(("dp", "ctx")),
            P(("dp", "ctx"), None),
            P(None, ("dp", "ctx")),
        ),
        check_vma=False,
    )
```
